256 devices in a mesh: stick: 16 (over y_lo, z), band: 16 (over x, y_hi, core).
Axes of the slice: x: 4, y: 4 (y_hi: 2, y_lo: 2; y = y_hi * 2 + y_lo), z: 8, core: 2. Of those that a mesh axis runs over, the one named last changes fastest.
Arguments:
- sticks: float32 [256, 96, 2048], P('band', None, 'stick'), may hold values from -0.0625 to 0.0625
- stick_columns: int32 [2048], P('stick'), may hold values from -1 to 2303, as said below
Outputs:
- exchange_sticks: float32 [256, 96, 2048], P('band', None, 'stick')
The draws below stay inside these ranges and needn't reach their ends.
Inputs may be any that keep to these rules, and one draw needn't show every extreme that they name: `stick_columns`: each entry is -1 (an empty slot) or a grid column kx * 48 + ky, and no column appears twice. On each index of the stick axis its 128 slots hold the live sticks first and the empty ones after; one index holds 128 live sticks, another 128 / 4, the others from 32 to 128.
All inputs are finite; a program needn't handle non-finite values.
Results may differ from the reference program's by a relative error of at most 0.0003.
Values sent between devices are 32-bit elements; how exact they have to be, the bound alone decides.
A program may use at most 64 MiB of HBM per device.

```python
import math
import jax
import jax.numpy as jnp
from jax import lax

G = 48
CAP = 128
HALF = 2
GROUPS = 16
GROUP_SIZE = 16
NBANDS = 256
STICKS = 2048


def draw_stick_columns(key, part):
    owner_count = STICKS // CAP
    key_order, key_count, key_full, key_light = jax.random.split(key, 4)
    column_order = jax.random.permutation(key_order, G * G).astype(jnp.int32)
    full_owner = jax.random.randint(key_full, (), 0, owner_count)
    light_owner = (full_owner + 1 + jax.random.randint(key_light, (), 0, owner_count - 1)) % owner_count
    last_column = G * G - 1
    last_place = jnp.argmax(column_order == last_column)
    target_slot = full_owner * CAP
    column_order = column_order.at[last_place].set(column_order[target_slot]).at[target_slot].set(last_column)
    owner_index = jnp.arange(owner_count)
    counts = jax.random.randint(key_count, (owner_count,), CAP // 4, CAP + 1)
    counts = jnp.where(owner_index == light_owner, CAP // 4, counts)
    counts = jnp.where(owner_index == full_owner, CAP, counts)
    slot_index = jnp.arange(STICKS)
    occupied = slot_index % CAP < counts[slot_index // CAP]
    return jnp.where(occupied, column_order[:STICKS], -1).astype(jnp.int32)


def block_scale(own_key, shape, cuts, least, largest):
    level = 1.0
    for dim, blocks in cuts:
        steps = jax.random.uniform(jax.random.fold_in(jax.random.fold_in(own_key, 6), dim), (blocks,), jnp.float32, least / len(cuts), largest / len(cuts))
        level = level * jnp.repeat(jnp.exp(steps), shape[dim] // blocks).reshape((-1,) + (1,) * (len(shape) - 1 - dim))
    return level


def centred(own_key, dims, spread, most, shards=(), kind=jnp.bfloat16):
    gain = block_scale(own_key, dims, shards, -0.22, 0.18) if shards else 1.0
    array = jax.random.normal(own_key, dims, jnp.float32) * spread * gain
    return jnp.minimum(jnp.maximum(array, -most), most).astype(kind)


def setup_inputs(seed: int = 0) -> dict:
    splits = jax.random.split(jax.random.key(seed), 3)
    sticks = centred(splits[0], (NBANDS, 2 * G, STICKS), ((1.6 / (STICKS * G)) ** 0.5), 0.0625, ((0, 16), (2, 16)), jnp.float32)
    stick_columns = draw_stick_columns(jax.random.fold_in(splits[2], 71), 0)
    return {"sticks": sticks, "stick_columns": stick_columns}


BOX_LENGTH = 18.0


def coulomb_kernel():
    half_count = G // 2 + 1
    frequency = jnp.arange(G, dtype=jnp.int32)
    folded = jnp.minimum(frequency, G - frequency)
    squares = folded * folded
    squared_sum = squares[:half_count, None, None] + squares[None, :, None] + squares[None, None, :]
    unit_square = (2.0 * math.pi / BOX_LENGTH) ** 2
    bounded = jnp.maximum(squared_sum, 1).astype(jnp.float32)
    return jnp.where(squared_sum > 0, 4.0 * math.pi / (unit_square * bounded), 0.0).astype(jnp.float32)


def orbital_field(band_rows, slot_rows):
    values = band_rows[:, :G] + 1j * band_rows[:, G:]
    grid = jnp.zeros((G * G + 1, G), values.dtype).at[slot_rows].set(values)[: G * G]
    return jnp.real(jnp.fft.ifftn(grid.reshape(G, G, G))) * float(G ** 3)


def potential(density, kernel):
    spectrum = jnp.fft.rfftn(density, axes=(2, 1, 0))
    return jnp.fft.irfftn(kernel * spectrum, s=(G, G, G), axes=(2, 1, 0))


def reference(sticks, stick_columns):
    slot_rows = jnp.where(stick_columns >= 0, stick_columns, G * G).astype(jnp.int32)
    kernel = coulomb_kernel()
    fields = lax.map(lambda band_rows: orbital_field(jnp.transpose(band_rows), slot_rows), sticks)
    fields = fields.reshape(GROUPS, GROUP_SIZE, G, G, G)

    def exchange_band(band_index):
        group_index = band_index // GROUP_SIZE
        member = band_index % GROUP_SIZE
        own_field = fields[group_index, member]
        exchange_sum = jnp.zeros((G, G, G), own_field.dtype)
        for offset in range(-HALF, HALF + 1):
            source = fields[(group_index + offset) % GROUPS, member]
            exchange_sum = exchange_sum + potential(own_field * source, kernel) * source
        spectrum = jnp.fft.fftn(exchange_sum) * (G ** -1.5)
        padded = jnp.concatenate([spectrum.reshape(G * G, G), jnp.zeros((1, G), spectrum.dtype)], axis=0)
        picked = padded[slot_rows]
        return jnp.transpose(jnp.concatenate([jnp.real(picked), jnp.imag(picked)], axis=1))

    return lax.map(exchange_band, jnp.arange(NBANDS, dtype=jnp.int32))
```

```python
import functools
import math

import jax
import jax.numpy as jnp
import ml_dtypes
import numpy as np
from jax import lax
from jax.experimental import pallas as pl
from jax.experimental.pallas import tpu as pltpu
from jax.sharding import PartitionSpec as P

G = 48
LANES = G * G
OWNERS = 16
CAP = 128
BOX_LENGTH = 18.0
F32, BF16 = jnp.float32, jnp.bfloat16


def two_parts(table):
    high = table.astype(ml_dtypes.bfloat16)
    low = (table - high.astype(np.float64)).astype(ml_dtypes.bfloat16)
    return high, low


def stacked(table):
    high, low = two_parts(table)
    return np.concatenate([high, high, low], axis=1)


def make_tables():
    index = np.arange(G)
    angle = 2.0 * np.pi / G * (np.outer(index, index) % G)
    cos, sin = np.cos(angle), np.sin(angle)
    plus = (cos + sin) / np.sqrt(G)
    minus = (cos - sin) / np.sqrt(G)
    on_y = np.kron(plus, np.eye(16))
    on_z = np.einsum("aibj,kl->akiblj", plus.reshape(3, 16, 3, 16), np.eye(8)).reshape(384, 384)
    folded = np.minimum(index, G - index).astype(np.float64) ** 2
    total = folded[:, None, None] + folded[None, :, None] + folded[None, None, :]
    kernel = np.where(total > 0, 4.0 * np.pi / ((2.0 * np.pi / BOX_LENGTH) ** 2 * np.maximum(total, 1.0)), 0.0)
    kernel = kernel.reshape(G, 6, 8, 3, 16).transpose(0, 3, 1, 2, 4).reshape(G, LANES)
    z_in = np.block([[cos, -sin], [sin, cos]])
    z_out = np.block([[cos, sin], [-sin, cos]]) * G**-1.5
    return dict(
        x=stacked(plus),
        x_in=stacked(np.concatenate([plus, minus], axis=1) * (0.5 * G)),
        x_out=stacked(np.concatenate([plus, minus], axis=0) * (0.5 * G)),
        y_high=two_parts(on_y)[0],
        y_low=two_parts(on_y)[1],
        z_high=two_parts(on_z)[0],
        z_low=two_parts(on_z)[1],
        kernel=kernel.astype(np.float32),
        z_in=stacked(z_in),
        z_out=stacked(z_out),
    )


TABLES = make_tables()


def dot(left, right):
    return jnp.dot(left, right, preferred_element_type=F32)


def split(value):
    high = value.astype(BF16)
    return high, (value - high.astype(F32)).astype(BF16)


def left_product(table, value):
    high, low = split(value)
    return dot(table, jnp.concatenate([high, low, high], axis=0))


def right_product(value, high_table, low_table):
    high, low = split(value)
    return dot(high, high_table) + dot(low, high_table) + dot(high, low_table)


def y_stage(fields, high, low):
    rows = [f[:, 768 * z : 768 * (z + 1)] for f in fields for z in range(3)]
    out = right_product(jnp.concatenate(rows, axis=0), high, low)
    pieces = [out[G * i : G * (i + 1)] for i in range(len(rows))]
    return [jnp.concatenate(pieces[3 * i : 3 * i + 3], axis=1) for i in range(len(fields))]


def tile(field, z, y):
    start = 128 * (6 * z + y)
    return field[:, start : start + 128]


def z_stage(fields, high, low):
    rows = [jnp.concatenate([tile(f, z, y) for z in range(3)], axis=1) for f in fields for y in range(6)]
    out = right_product(jnp.concatenate(rows, axis=0), high, low)
    pieces = [out[G * i : G * (i + 1)] for i in range(len(rows))]
    return [
        jnp.concatenate([pieces[6 * i + y][:, 128 * z : 128 * (z + 1)] for z in range(3) for y in range(6)], axis=1)
        for i in range(len(fields))
    ]


def reflected(tiles):
    lane = lax.broadcasted_iota(jnp.int32, (G, 128), 1) // 16
    out = []
    for y in range(6):
        source = tiles[5 - y]
        turned = jnp.where(
            lane == 4,
            source,
            jnp.where(
                lane % 4 == 1,
                pltpu.roll(source, 32, 1),
                jnp.where(lane % 4 == 2, pltpu.roll(source, 64, 1), pltpu.roll(source, 96, 1)),
            ),
        )
        out.append(jnp.where(lane == 0, tiles[(6 - y) % 6], turned))
    return out


def slot_places(columns):
    kx = (columns * 43691) >> 21
    ky = columns - kx * G
    row = (ky >> 3) * G + kx
    return jnp.where(columns >= 0, row, -1), ky & 7


def one_hot(row):
    places = lax.broadcasted_iota(jnp.int32, (6 * G, CAP), 0)
    return jnp.where(places == row, 1.0, 0.0).astype(BF16)


def in_kernel(blocks, x_in, y_high, y_low, z_in, orbital):
    groups = lax.broadcasted_iota(jnp.int32, (128, CAP), 0) >> 4

    def place(owner, grid):
        values = blocks[owner, : 2 * G, :]
        columns = blocks[owner, 2 * G : 2 * G + 1, :].astype(jnp.int32)
        row, group = slot_places(columns)
        high, low = split(left_product(z_in[...], values))
        keep = jnp.where(groups == group, 1.0, 0.0).astype(BF16)
        spread = [
            jnp.concatenate([jnp.concatenate([part[16 * t : 16 * t + 16]] * 8, axis=0) * keep for t in range(6)], axis=0)
            for part in (high, low)
        ]
        hot = one_hot(row)
        return grid + lax.dot_general(
            jnp.concatenate([hot, hot], axis=1),
            jnp.concatenate(spread, axis=1),
            (((1,), (1,)), ((), ())),
            preferred_element_type=F32,
        )

    grid = lax.fori_loop(0, OWNERS, place, jnp.zeros((6 * G, 768), F32))

    def tiles(t):
        return [grid[G * y : G * (y + 1), 128 * t : 128 * (t + 1)] for y in range(6)]

    first, second = [], []
    for z in range(3):
        real, imag = tiles(z), tiles(3 + z)
        first += [r - i for r, i in zip(reflected(real), imag)]
        second += [r + i for r, i in zip(real, reflected(imag))]
    pair = y_stage([jnp.concatenate(first, axis=1), jnp.concatenate(second, axis=1)], y_high[...], y_low[...])
    orbital[...] = left_product(x_in[...], jnp.concatenate(pair, axis=0))


def pot_kernel(count, own, *refs):
    sources, (x, y_high, y_low, z_high, z_low, kernel, start, out) = refs[:count], refs[count:]
    fields = [left_product(x[...], own[...] * s[...]) for s in sources]
    fields = y_stage(fields, y_high[...], y_low[...])
    fields = z_stage(fields, z_high[...], z_low[...])
    fields = [f * kernel[...] for f in fields]
    fields = z_stage(fields, z_high[...], z_low[...])
    fields = y_stage(fields, y_high[...], y_low[...])
    total = start[...]
    for f, s in zip(fields, sources):
        total = total + left_product(x[...], f) * s[...]
    out[...] = total


def out_kernel(field, columns, x_out, y_high, y_low, z_out, out, turned):
    pair = left_product(x_out[...], field[...])
    plus, minus = y_stage([pair[:G], pair[G:]], y_high[...], y_low[...])
    real, imag = [], []
    for z in range(3):
        p = [tile(plus, z, y) for y in range(6)]
        m = [tile(minus, z, y) for y in range(6)]
        real.append([a + b for a, b in zip(m, reflected(p))])
        imag.append([a - b for a, b in zip(reflected(m), p)])
    for t, part in enumerate(real + imag):
        column = jnp.concatenate(part + [jnp.zeros((96, 128), F32)], axis=0)
        high, low = split(column.T[:, : 6 * G])
        turned[0, 128 * t : 128 * (t + 1), :] = high
        turned[1, 128 * t : 128 * (t + 1), :] = low
    groups = lax.broadcasted_iota(jnp.int32, (8, CAP), 0)

    def pick(owner, carry):
        row, group = slot_places(columns[owner, :, :].astype(jnp.int32))
        hot = one_hot(row)
        found = dot(turned[0], hot) + dot(turned[1], hot)
        rows = []
        for t in range(6):
            total = jnp.zeros((16, CAP), F32)
            for g in range(8):
                start = 128 * t + 16 * g
                total = total + jnp.where(group == g, found[start : start + 16], 0.0)
            rows.append(total)
        out[owner, :, :] = left_product(z_out[...], jnp.concatenate(rows, axis=0))
        return carry

    lax.fori_loop(0, OWNERS, pick, 0)


def call(kernel, out_shape, args, scratch=(), flops=1e9):
    return pl.pallas_call(
        kernel,
        out_shape=jax.ShapeDtypeStruct(out_shape, F32),
        in_specs=[pl.BlockSpec(memory_space=pltpu.VMEM)] * len(args),
        out_specs=pl.BlockSpec(memory_space=pltpu.VMEM),
        scratch_shapes=list(scratch),
        cost_estimate=pl.CostEstimate(flops=int(flops), bytes_accessed=int(4e6), transcendentals=0),
    )(*args)


def orbital_of(blocks, t):
    return call(in_kernel, (G, LANES), [blocks, t["x_in"], t["y_high"], t["y_low"], t["z_in"]])


def add_pots(own, sources, start, t):
    names = ("x", "y_high", "y_low", "z_high", "z_low", "kernel")
    return call(
        functools.partial(pot_kernel, len(sources)), (G, LANES), [own, *sources, *(t[n] for n in names), start], flops=3e9 * len(sources)
    )


def exchange_of(field, columns, t):
    return call(
        out_kernel,
        (OWNERS, 2 * G, CAP),
        [field, columns, t["x_out"], t["y_high"], t["y_low"], t["z_out"]],
        [pltpu.VMEM((2, 768, 6 * G), BF16)],
    )


def passed_along(shard, axis, by):
    size = lax.axis_size(axis)
    return lax.ppermute(shard, axis, [(i, (i + by) % size) for i in range(size)])


def on_device(sticks, stick_columns):
    t = {name: jnp.asarray(value) for name, value in TABLES.items()}
    labels = jnp.broadcast_to(stick_columns.astype(F32), (OWNERS, 8, CAP))
    sent = jnp.concatenate([sticks, labels], axis=1)
    blocks = lax.all_to_all(sent, "stick", split_axis=0, concat_axis=0, tiled=True)
    orbital = orbital_of(blocks, t)
    near = [passed_along(orbital, "band", by) for by in (1, -1)]
    far = [passed_along(orbital, "band", by) for by in (2, -2)]
    field = add_pots(orbital, [orbital], jnp.zeros((G, LANES), F32), t)
    field = add_pots(orbital, near, field, t)
    field = add_pots(orbital, far, field, t)
    columns = blocks[:, 2 * G : 2 * G + 1, :]
    result = exchange_of(field, columns, t)
    return lax.all_to_all(result, "stick", split_axis=0, concat_axis=0, tiled=True)


def solution(mesh):
    return jax.shard_map(
        on_device,
        mesh=mesh,
        in_specs=(P("band", None, "stick"), P("stick")),
        out_specs=P("band", None, "stick"),
        check_vma=False,
    )
```

```python
import functools
import math

import jax
import jax.numpy as jnp
import ml_dtypes
import numpy as np
from jax import lax
from jax.experimental import pallas as pl
from jax.experimental.pallas import tpu as pltpu
from jax.sharding import PartitionSpec as P

G = 48
ROWS, WIDE = 3 * G, 16 * G
OWNERS = 16
CAP = 128
BOX_LENGTH = 18.0
F32, BF16 = jnp.float32, jnp.bfloat16


def two_parts(table):
    high = table.astype(ml_dtypes.bfloat16)
    low = (table - high.astype(np.float64)).astype(ml_dtypes.bfloat16)
    return high, low


def stacked(table):
    high, low = two_parts(table)
    return np.concatenate([high, high, low], axis=1)


def make_tables():
    index = np.arange(G)
    angle = 2.0 * np.pi / G * (np.outer(index, index) % G)
    cos, sin = np.cos(angle), np.sin(angle)
    plus = (cos + sin) / np.sqrt(G)
    minus = (cos - sin) / np.sqrt(G)
    on_y = np.kron(plus, np.eye(16))
    on_z = np.einsum("aibj,kl->akiblj", plus.reshape(3, 16, 3, 16), np.eye(8)).reshape(384, 384)
    folded = np.minimum(index, G - index).astype(np.float64) ** 2
    total = folded[:, None, None] + folded[None, :, None] + folded[None, None, :]
    kernel = np.where(total > 0, 4.0 * np.pi / ((2.0 * np.pi / BOX_LENGTH) ** 2 * np.maximum(total, 1.0)), 0.0)
    kernel = kernel.reshape(G, 6, 8, 3, 16).transpose(3, 0, 1, 2, 4).reshape(ROWS, WIDE)
    z_in = np.block([[cos, -sin], [sin, cos]])
    z_out = np.block([[cos, sin], [-sin, cos]]) * G**-1.5
    return dict(
        x=stacked(plus),
        x_in=stacked(np.concatenate([plus, minus], axis=1) * (0.5 * G)),
        x_out=stacked(np.concatenate([plus, minus], axis=0) * (0.5 * G)),
        y_high=two_parts(on_y)[0],
        y_low=two_parts(on_y)[1],
        z_high=two_parts(on_z)[0],
        z_low=two_parts(on_z)[1],
        kernel=kernel.astype(np.float32),
        z_in=stacked(z_in),
        z_out=stacked(z_out),
    )


TABLES = make_tables()


def dot(left, right):
    return jnp.dot(left, right, preferred_element_type=F32)


def split(value):
    high = value.astype(BF16)
    return high, (value - high.astype(F32)).astype(BF16)


def left_product(table, value):
    high, low = split(value)
    return dot(table, jnp.concatenate([high, low, high], axis=0))


def right_product(value, high_table, low_table):
    high, low = split(value)
    return dot(high, high_table) + dot(low, high_table) + dot(high, low_table)


MESH = pl.DeviceIdType.MESH
STAGES = tuple(TABLES)


def chip_of(pair):
    place = (pair + 6) % 8
    row = place // 4
    return place + row * (7 - 2 * place), row


def computer_of(pair, core, member):
    x, row = chip_of(pair)
    return row * 8 + member % 8, x * 4 + member // 8 * 2 + core


def role_of(stick, band):
    row, x = stick // 8, band // 4
    place = x + row * (7 - 2 * x)
    return (place + 2) % 8, band % 2, band % 4 // 2 * 8 + stick % 8


def hop_of(step):
    return 2 + (step + 1) // 2 * (1 - 2 * (step % 2))


def member_at(step, stick):
    half, rest = step // 8, step % 8
    return rest % 2 * 8 + (stick % 8 // 2 + hop_of(rest // 2)) % 4 * 2 + half


def owner_at(step, member):
    return step % 2 * 8 + (member % 8 // 2 + 8 - hop_of(step // 4)) % 4 * 2 + step // 2 % 2


def y_stage(field, high, low):
    return right_product(field, high, low)


def z_stage(field, high, low):
    rows = [
        jnp.concatenate([field[G * z : G * (z + 1), 128 * y : 128 * (y + 1)] for z in range(3)], axis=1) for y in range(6)
    ]
    out = right_product(jnp.concatenate(rows, axis=0), high, low)
    return jnp.concatenate(
        [
            jnp.concatenate([out[G * y : G * (y + 1), 128 * z : 128 * (z + 1)] for y in range(6)], axis=1)
            for z in range(3)
        ],
        axis=0,
    )


def x_stage(field, table):
    return jnp.concatenate([left_product(table, field[G * z : G * (z + 1)]) for z in range(3)], axis=0)


def reflected(tiles):
    lane = lax.broadcasted_iota(jnp.int32, (G, 128), 1) // 16
    out = []
    for y in range(6):
        source = tiles[5 - y]
        turned = jnp.where(
            lane == 4,
            source,
            jnp.where(
                lane % 4 == 1,
                pltpu.roll(source, 32, 1),
                jnp.where(lane % 4 == 2, pltpu.roll(source, 64, 1), pltpu.roll(source, 96, 1)),
            ),
        )
        out.append(jnp.where(lane == 0, tiles[(6 - y) % 6], turned))
    return out


def slot_places(columns):
    kx = (columns * 43691) >> 21
    ky = columns - kx * G
    row = (ky >> 3) * G + kx
    return jnp.where(columns >= 0, row, -1), ky & 7


def one_hot(row):
    places = lax.broadcasted_iota(jnp.int32, (6 * G, CAP), 0)
    return jnp.where(places == row, 1.0, 0.0).astype(BF16)


def exchange_kernel(sticks, labels, *refs):
    count = len(STAGES)
    stored, out, held = refs[:count], refs[count], refs[count + 1 : 2 * count + 1]
    t = dict(zip(STAGES, held))
    (blocks, columns, grid, fields, total, turned, found, table_sem, in_send, in_recv, label_send, label_recv,
     field_send, field_recv, out_send, out_recv) = refs[2 * count + 1 :]
    stick, band = lax.axis_index("stick"), lax.axis_index("band")
    pair, core, member = role_of(stick, band)
    group = 2 * pair + core

    loads = [pltpu.make_async_copy(a, b, table_sem.at[i]) for i, (a, b) in enumerate(zip(stored, held))]
    for load in loads:
        load.start()

    def own_computer(member):
        return computer_of(band // 2, band % 2, member)

    def mine(device):
        return jnp.logical_and(device[0] == stick, device[1] == band)

    upper, lower = (pair + 1) % 8, (pair + 7) % 8
    to_upper, to_lower = computer_of(upper, 0, member), computer_of(lower, 1, member)
    partner = computer_of(pair, 1 - core, member)
    beyond = core * upper + (1 - core) * lower
    from_first, from_second = computer_of(beyond, 0, member), computer_of(beyond, 1, member)

    barrier = pltpu.get_barrier_semaphore()

    def signal(device):
        pl.semaphore_signal(barrier, 1, device_id=device, device_id_type=MESH)

    def greet(i, carry):
        for device in ((i, group), own_computer(i)):

            @pl.when(jnp.logical_not(mine(device)))
            def _():
                signal(device)

        return carry

    lax.fori_loop(0, OWNERS, greet, 0)
    for device in (from_first, from_second, partner):
        signal(device)

    pl.semaphore_wait(barrier, 2 * OWNERS + 3 - 2 * jnp.where(group == band, 1, 0))

    def stick_copies(i):
        device = own_computer(i)
        pairs = (
            (sticks.at[i], blocks.at[stick], in_send.at[i], in_recv.at[stick]),
            (labels, columns.at[stick], label_send.at[i], label_recv.at[stick]),
        )
        local = [pltpu.make_async_copy(a, b, r) for a, b, s, r in pairs]
        remote = [
            pltpu.make_async_remote_copy(a, b, s, r, device_id=device, device_id_type=MESH) for a, b, s, r in pairs
        ]
        return mine(device), local, remote

    def send(step, carry):
        here, local, remote = stick_copies(member_at(step, stick))

        @pl.when(here)
        def _():
            for copy in local:
                copy.start()

        @pl.when(jnp.logical_not(here))
        def _():
            for copy in remote:
                copy.start()

        return carry

    lax.fori_loop(0, OWNERS, send, 0)

    grid[...] = jnp.zeros_like(grid)
    for load in loads:
        load.wait()
    spans = lax.broadcasted_iota(jnp.int32, (128, CAP), 0) >> 4

    def place(step, carry):
        owner = owner_at(step, member)
        pltpu.make_async_copy(blocks.at[owner], blocks.at[owner], in_recv.at[owner]).wait()
        pltpu.make_async_copy(columns.at[owner], columns.at[owner], label_recv.at[owner]).wait()
        row, span = slot_places(columns[owner])
        high, low = split(left_product(t["z_in"][...], blocks[owner]))
        keep = jnp.where(spans == span, 1.0, 0.0).astype(BF16)
        spread = [
            jnp.concatenate([jnp.concatenate([part[16 * i : 16 * i + 16]] * 8, axis=0) * keep for i in range(6)], axis=0)
            for part in (high, low)
        ]
        hot = one_hot(row)
        grid[...] += lax.dot_general(
            jnp.concatenate([hot, hot], axis=1),
            jnp.concatenate(spread, axis=1),
            (((1,), (1,)), ((), ())),
            preferred_element_type=F32,
        )
        return carry

    lax.fori_loop(0, OWNERS, place, 0)

    def tiles(i):
        return [grid[G * y : G * (y + 1), 128 * i : 128 * (i + 1)] for y in range(6)]

    first, second = [], []
    for z in range(3):
        real, imag = tiles(z), tiles(3 + z)
        first.append(jnp.concatenate([a - b for a, b in zip(reflected(real), imag)], axis=1))
        second.append(jnp.concatenate([a + b for a, b in zip(real, reflected(imag))], axis=1))
    both = y_stage(jnp.concatenate(first + second, axis=0), t["y_high"][...], t["y_low"][...])
    for z in range(3):
        rows = jnp.concatenate([both[G * z : G * (z + 1)], both[ROWS + G * z : ROWS + G * (z + 1)]], axis=0)
        fields[0, G * z : G * (z + 1), :] = left_product(t["x_in"][...], rows)

    def field_copy(source, slot, index, device):
        return pltpu.make_async_remote_copy(
            fields.at[source], fields.at[slot], field_send.at[index], field_recv.at[slot], device_id=device, device_id_type=MESH
        )

    outward = [field_copy(0, 2 + core, 0, to_upper), field_copy(0, 2 + core, 1, to_lower), field_copy(0, 1, 2, partner)]
    for copy in outward:
        copy.start()
    onward = field_copy(3 - core, 4, 3, partner)

    def arrive(slot):
        pltpu.make_async_copy(fields.at[slot], fields.at[slot], field_recv.at[slot]).wait()

    total[...] = jnp.zeros_like(total)

    def pot(slot, carry):
        @pl.when(slot == 1)
        def _():
            arrive(1)

        @pl.when(slot == 2)
        def _():
            arrive(2)
            arrive(3)
            onward.start()

        @pl.when(slot == 4)
        def _():
            arrive(4)

        value = x_stage(fields[0] * fields[slot], t["x"][...])
        value = y_stage(value, t["y_high"][...], t["y_low"][...])
        value = z_stage(value, t["z_high"][...], t["z_low"][...])
        value = value * t["kernel"][...]
        value = z_stage(value, t["z_high"][...], t["z_low"][...])
        value = y_stage(value, t["y_high"][...], t["y_low"][...])
        total[...] += x_stage(value, t["x"][...]) * fields[slot]
        return carry

    lax.fori_loop(0, 5, pot, 0)
    for copy in outward:
        copy.wait_send()
    onward.wait_send()

    split_x = [left_product(t["x_out"][...], total[G * z : G * (z + 1), :]) for z in range(3)]
    both = y_stage(
        jnp.concatenate([v[:G] for v in split_x] + [v[G:] for v in split_x], axis=0), t["y_high"][...], t["y_low"][...]
    )

    def out_tiles(i):
        return [both[G * i : G * (i + 1), 128 * y : 128 * (y + 1)] for y in range(6)]

    real, imag = [], []
    for z in range(3):
        plus, minus = out_tiles(z), out_tiles(3 + z)
        real.append([a + b for a, b in zip(minus, reflected(plus))])
        imag.append([a - b for a, b in zip(reflected(minus), plus)])
    for i, part in enumerate(real + imag):
        column = jnp.concatenate(part + [jnp.zeros((96, 128), F32)], axis=0)
        high, low = split(column.T[:, : 6 * G])
        turned[0, 128 * i : 128 * (i + 1), :] = high
        turned[1, 128 * i : 128 * (i + 1), :] = low

    def result_copies(owner):
        device = (owner, group)
        local = pltpu.make_async_copy(found.at[owner], out.at[member], out_recv.at[member])
        remote = pltpu.make_async_remote_copy(
            found.at[owner], out.at[member], out_send.at[owner], out_recv.at[member], device_id=device, device_id_type=MESH
        )
        return mine(device), local, remote

    def pick(step, carry):
        owner = owner_at(step, member)
        row, span = slot_places(columns[owner])
        hot = one_hot(row)
        picked = dot(turned[0], hot) + dot(turned[1], hot)
        rows = []
        for i in range(6):
            value = jnp.zeros((16, CAP), F32)
            for g in range(8):
                start = 128 * i + 16 * g
                value = value + jnp.where(span == g, picked[start : start + 16], 0.0)
            rows.append(value)
        found[owner] = left_product(t["z_out"][...], jnp.concatenate(rows, axis=0))
        here, local, remote = result_copies(owner)

        @pl.when(here)
        def _():
            local.start()

        @pl.when(jnp.logical_not(here))
        def _():
            remote.start()

        return carry

    lax.fori_loop(0, OWNERS, pick, 0)

    def finish(i, carry):
        here, _, remote = stick_copies(i)

        @pl.when(jnp.logical_not(here))
        def _():
            for copy in remote:
                copy.wait_send()

        here, _, remote = result_copies(i)

        @pl.when(jnp.logical_not(here))
        def _():
            remote.wait_send()

        pltpu.make_async_copy(out.at[i], out.at[i], out_recv.at[i]).wait()
        return carry

    lax.fori_loop(0, OWNERS, finish, 0)


def on_device(sticks, stick_columns):
    tables = [jnp.asarray(TABLES[name]) for name in STAGES]
    anywhere = pl.BlockSpec(memory_space=pl.ANY)
    dma = pltpu.SemaphoreType.DMA
    return pl.pallas_call(
        exchange_kernel,
        out_shape=jax.ShapeDtypeStruct((OWNERS, 2 * G, CAP), F32),
        in_specs=[anywhere, pl.BlockSpec(memory_space=pltpu.VMEM)] + [anywhere] * len(tables),
        out_specs=anywhere,
        scratch_shapes=[pltpu.VMEM(t.shape, t.dtype) for t in tables]
        + [
            pltpu.VMEM((OWNERS, 2 * G, CAP), F32),
            pltpu.VMEM((OWNERS, 1, CAP), jnp.int32),
            pltpu.VMEM((6 * G, WIDE), F32),
            pltpu.VMEM((5, ROWS, WIDE), F32),
            pltpu.VMEM((ROWS, WIDE), F32),
            pltpu.VMEM((2, WIDE, 6 * G), BF16),
            pltpu.VMEM((OWNERS, 2 * G, CAP), F32),
            dma((len(tables),)),
        ]
        + [dma((OWNERS,))] * 4
        + [dma((4,)), dma((5,)), dma((OWNERS,)), dma((OWNERS,))],
        compiler_params=pltpu.CompilerParams(collective_id=0, has_side_effects=True, vmem_limit_bytes=56 << 20),
    )(sticks, stick_columns.reshape(1, CAP), *tables)


def solution(mesh):
    return jax.shard_map(
        on_device,
        mesh=mesh,
        in_specs=(P("band", None, "stick"), P("stick")),
        out_specs=P("band", None, "stick"),
        check_vma=False,
    )
```

```python
import functools
import math

import jax
import jax.numpy as jnp
import ml_dtypes
import numpy as np
from jax import lax
from jax.experimental import pallas as pl
from jax.experimental.pallas import tpu as pltpu
from jax.sharding import PartitionSpec as P

G = 48
ROWS, WIDE = 3 * G, 16 * G
OWNERS = 16
CAP = 128
BOX_LENGTH = 18.0
F32, BF16 = jnp.float32, jnp.bfloat16


def two_parts(table):
    high = table.astype(ml_dtypes.bfloat16)
    low = (table - high.astype(np.float64)).astype(ml_dtypes.bfloat16)
    return high, low


def stacked(table):
    high, low = two_parts(table)
    return np.concatenate([high, high, low], axis=1)


def make_tables():
    index = np.arange(G)
    angle = 2.0 * np.pi / G * (np.outer(index, index) % G)
    cos, sin = np.cos(angle), np.sin(angle)
    plus = (cos + sin) / np.sqrt(G)
    minus = (cos - sin) / np.sqrt(G)
    on_y = np.kron(plus, np.eye(16))
    on_z = np.einsum("aibj,kl->akiblj", plus.reshape(3, 16, 3, 16), np.eye(8)).reshape(384, 384)
    folded = np.minimum(index, G - index).astype(np.float64) ** 2
    total = folded[:, None, None] + folded[None, :, None] + folded[None, None, :]
    kernel = np.where(total > 0, 4.0 * np.pi / ((2.0 * np.pi / BOX_LENGTH) ** 2 * np.maximum(total, 1.0)), 0.0)
    kernel = kernel.reshape(G, 6, 8, 3, 16).transpose(3, 0, 1, 2, 4).reshape(ROWS, WIDE)
    z_in = np.block([[cos, -sin], [sin, cos]]).reshape(2, 3, 16, 2 * G).transpose(1, 0, 2, 3).reshape(2 * G, 2 * G)
    z_out = np.block([[cos, sin], [-sin, cos]])
    return dict(
        x=stacked(plus),
        x_in=stacked(np.concatenate([plus, minus], axis=1) * (0.5 * G)),
        x_out=stacked(np.concatenate([plus, minus], axis=0) * (0.5 * G)),
        y_high=two_parts(on_y)[0],
        y_low=two_parts(on_y)[1],
        z_high=two_parts(on_z)[0],
        z_low=two_parts(on_z)[1],
        kernel=kernel.astype(np.float32),
        z_in=stacked(z_in),
        z_out=stacked(z_out),
    )


TABLES = make_tables()


def dot(left, right):
    return jnp.dot(left, right, preferred_element_type=F32)


def split(value):
    high = value.astype(BF16)
    return high, (value - high.astype(F32)).astype(BF16)


def left_product(table, value):
    high, low = split(value)
    return dot(table, jnp.concatenate([high, low, high], axis=0))


def right_product(value, high_table, low_table):
    high, low = split(value)
    return dot(high, high_table) + dot(low, high_table) + dot(high, low_table)


MESH = pl.DeviceIdType.MESH
STAGES = tuple(TABLES)


def chip_of(pair):
    place = (pair + 6) % 8
    row = place // 4
    return place + row * (7 - 2 * place), row


def computer_of(pair, core, member):
    x, row = chip_of(pair)
    return row * 8 + member % 8, x * 4 + member // 8 * 2 + core


def role_of(stick, band):
    row, x = stick // 8, band // 4
    place = x + row * (7 - 2 * x)
    return (place + 2) % 8, band % 2, band % 4 // 2 * 8 + stick % 8


def y_stage(field, high, low):
    return right_product(field, high, low)


def z_stage(field, high, low):
    rows = [
        jnp.concatenate([field[G * z : G * (z + 1), 128 * y : 128 * (y + 1)] for z in range(3)], axis=1) for y in range(6)
    ]
    out = right_product(jnp.concatenate(rows, axis=0), high, low)
    return jnp.concatenate(
        [
            jnp.concatenate([out[G * y : G * (y + 1), 128 * z : 128 * (z + 1)] for y in range(6)], axis=1)
            for z in range(3)
        ],
        axis=0,
    )


def x_stage(field, table):
    return jnp.concatenate([left_product(table, field[G * z : G * (z + 1)]) for z in range(3)], axis=0)


def reflected(tiles):
    lane = lax.broadcasted_iota(jnp.int32, (G, 128), 1) // 16
    out = []
    for y in range(6):
        source = tiles[5 - y]
        turned = jnp.where(
            lane == 4,
            source,
            jnp.where(
                lane % 4 == 1,
                pltpu.roll(source, 32, 1),
                jnp.where(lane % 4 == 2, pltpu.roll(source, 64, 1), pltpu.roll(source, 96, 1)),
            ),
        )
        out.append(jnp.where(lane == 0, tiles[(6 - y) % 6], turned))
    return out


def slot_places(columns):
    kx = (columns * 43691) >> 21
    ky = columns - kx * G
    row = (ky >> 3) * G + kx
    return jnp.where(columns >= 0, row, -1), ky & 7


def one_hot(row):
    places = lax.broadcasted_iota(jnp.int32, (6 * G, row.shape[1]), 0)
    return jnp.where(places == row, 1.0, 0.0).astype(BF16)


def exchange_kernel(sticks, labels, *refs):
    count = len(STAGES)
    stored, out, held = refs[:count], refs[count], refs[count + 1 : 2 * count + 1]
    t = dict(zip(STAGES, held))
    (sent, blocks, columns, grid, fields, total, turned, found, table_sem, in_send, in_recv, label_send, label_recv,
     field_send, field_recv, out_send, out_recv) = refs[2 * count + 1 :]
    stick, band = lax.axis_index("stick"), lax.axis_index("band")
    pair, core, member = role_of(stick, band)
    group = 2 * pair + core

    loads = [pltpu.make_async_copy(a, b, table_sem.at[i]) for i, (a, b) in enumerate(zip(stored, held))]
    for load in loads:
        load.start()

    def own_computer(member):
        return computer_of(band // 2, band % 2, member)

    def mine(device):
        return jnp.logical_and(device[0] == stick, device[1] == band)

    upper, lower = (pair + 1) % 8, (pair + 7) % 8
    to_upper, to_lower = computer_of(upper, 0, member), computer_of(lower, 1, member)
    partner = computer_of(pair, 1 - core, member)
    beyond = core * upper + (1 - core) * lower
    from_first, from_second = computer_of(beyond, 0, member), computer_of(beyond, 1, member)

    barrier = pltpu.get_barrier_semaphore()

    def signal(device):
        pl.semaphore_signal(barrier, 1, device_id=device, device_id_type=MESH)

    def greet(i, carry):
        for device in ((i, group), own_computer(i)):

            @pl.when(jnp.logical_not(mine(device)))
            def _():
                signal(device)

        return carry

    lax.fori_loop(0, OWNERS, greet, 0)
    for device in (from_first, from_second, partner):
        signal(device)

    for load in loads:
        load.wait()

    def to_planes(i, carry):
        sent[i] = left_product(t["z_in"][...], sticks[i])
        return carry

    lax.fori_loop(0, OWNERS, to_planes, 0)
    pl.semaphore_wait(barrier, 2 * OWNERS + 3 - 2 * jnp.where(group == band, 1, 0))

    def either(device, source, target, out_sem, in_sem, start):
        @pl.when(mine(device))
        def _():
            if start:
                pltpu.make_async_copy(source, target, in_sem).start()

        @pl.when(jnp.logical_not(mine(device)))
        def _():
            copy = pltpu.make_async_remote_copy(
                source, target, out_sem, in_sem, device_id=device, device_id_type=MESH
            )
            if start:
                copy.start()
            else:
                copy.wait_send()

    def label_copy(i, start):
        either(own_computer(i), labels, columns.at[stick], label_send.at[i], label_recv.at[stick], start)

    def plane_copy(z, i, start):
        source, target = sent.at[i, pl.ds(pl.multiple_of(32 * z, 32), 32)], blocks.at[z, stick]
        either(own_computer(i), source, target, in_send.at[z, i], in_recv.at[z, stick], start)

    def send_labels(step, carry):
        label_copy((stick + step) % OWNERS, True)
        return carry

    def send_planes(index, carry):
        plane_copy(index // OWNERS, (stick + index) % OWNERS, True)
        return carry

    lax.fori_loop(0, OWNERS, send_labels, 0)
    lax.fori_loop(0, 3 * OWNERS, send_planes, 0)

    spans = lax.broadcasted_iota(jnp.int32, (128, CAP), 0) >> 4

    def arrive(ref, sem):
        pltpu.make_async_copy(ref, ref, sem).wait()

    def field_copy(source, slot, z, index, device):
        return pltpu.make_async_remote_copy(
            fields.at[source, z],
            fields.at[slot, z],
            field_send.at[index, z],
            field_recv.at[slot, z],
            device_id=device,
            device_id_type=MESH,
        )

    def outward(z):
        return [
            field_copy(0, 2 + core, z, 0, to_upper),
            field_copy(0, 2 + core, z, 1, to_lower),
            field_copy(0, 1, z, 2, partner),
        ]

    def onward(z):
        return field_copy(3 - core, 4, z, 3, partner)

    def plane(z, carry):
        grid[...] = jnp.zeros_like(grid)

        def place(step, carry):
            owner = (member + OWNERS - step) % OWNERS

            @pl.when(z == 0)
            def _():
                arrive(columns.at[owner], label_recv.at[owner])

            arrive(blocks.at[z, owner], in_recv.at[z, owner])
            row, span = slot_places(columns[owner])
            high, low = split(blocks[z, owner])
            keep = jnp.where(spans == span, 1.0, 0.0).astype(BF16)
            spread = [
                jnp.concatenate([jnp.concatenate([part[16 * i : 16 * i + 16]] * 8, axis=0) * keep for i in range(2)], axis=0)
                for part in (high, low)
            ]
            hot = one_hot(row)
            grid[...] += lax.dot_general(
                jnp.concatenate([hot, hot], axis=1),
                jnp.concatenate(spread, axis=1),
                (((1,), (1,)), ((), ())),
                preferred_element_type=F32,
            )
            return carry

        lax.fori_loop(0, OWNERS, place, 0)
        real = [grid[G * y : G * (y + 1), :128] for y in range(6)]
        imag = [grid[G * y : G * (y + 1), 128:] for y in range(6)]
        first = jnp.concatenate([a - b for a, b in zip(reflected(real), imag)], axis=1)
        second = jnp.concatenate([a + b for a, b in zip(real, reflected(imag))], axis=1)
        both = y_stage(jnp.concatenate([first, second], axis=0), t["y_high"][...], t["y_low"][...])
        fields[0, z] = left_product(t["x_in"][...], both)
        for copy in outward(z):
            copy.start()

        @pl.when(z > 0)
        def _():
            arrive(fields.at[3 - core, z - 1], field_recv.at[3 - core, z - 1])
            onward(z - 1).start()

        return carry

    lax.fori_loop(0, 3, plane, 0)
    total[...] = jnp.zeros_like(total)

    def arrive_field(slot):
        for z in range(3):
            arrive(fields.at[slot, z], field_recv.at[slot, z])

    def pot(slot, carry):
        @pl.when(slot == 1)
        def _():
            arrive_field(1)

        @pl.when(slot == 2)
        def _():
            arrive(fields.at[3 - core, 2], field_recv.at[3 - core, 2])
            onward(2).start()
            arrive_field(2 + core)

        @pl.when(slot == 4)
        def _():
            arrive_field(4)

        source = fields[slot].reshape(ROWS, WIDE)
        value = x_stage(fields[0].reshape(ROWS, WIDE) * source, t["x"][...])
        value = y_stage(value, t["y_high"][...], t["y_low"][...])
        value = z_stage(value, t["z_high"][...], t["z_low"][...])
        value = value * t["kernel"][...]
        value = z_stage(value, t["z_high"][...], t["z_low"][...])
        value = y_stage(value, t["y_high"][...], t["y_low"][...])
        total[...] += x_stage(value, t["x"][...]) * source
        return carry

    lax.fori_loop(0, 5, pot, 0)
    for z in range(3):
        for copy in outward(z):
            copy.wait_send()
        onward(z).wait_send()

    split_x = [left_product(t["x_out"][...], total[G * z : G * (z + 1), :]) for z in range(3)]
    both = y_stage(
        jnp.concatenate([v[:G] for v in split_x] + [v[G:] for v in split_x], axis=0), t["y_high"][...], t["y_low"][...]
    )

    def out_tiles(i):
        return [both[G * i : G * (i + 1), 128 * y : 128 * (y + 1)] for y in range(6)]

    real, imag = [], []
    for z in range(3):
        plus, minus = out_tiles(z), out_tiles(3 + z)
        real.append([a + b for a, b in zip(minus, reflected(plus))])
        imag.append([a - b for a, b in zip(reflected(minus), plus)])
    for i, part in enumerate(real + imag):
        column = jnp.concatenate(part + [jnp.zeros((96, 128), F32)], axis=0)
        high, low = split(column.T[:, : 6 * G])
        turned[128 * i : 128 * (i + 1), : 6 * G] = high
        turned[128 * i : 128 * (i + 1), 6 * G :] = low

    def result_copy(owner, start):
        either((owner, group), found.at[owner], out.at[member], out_send.at[owner], out_recv.at[member], start)

    def pick(step, carry):
        owners = [(member + OWNERS - 2 * step - i) % OWNERS for i in range(2)]
        row, span = slot_places(jnp.concatenate([columns[owner] for owner in owners], axis=1))
        hot = one_hot(row)
        picked = dot(turned[...], jnp.concatenate([hot, hot], axis=0))
        rows = []
        for i in range(6):
            value = jnp.zeros((16, 2 * CAP), F32)
            for g in range(8):
                start = 128 * i + 16 * g
                value = value + jnp.where(span == g, picked[start : start + 16], 0.0)
            rows.append(value)
        result = left_product(t["z_out"][...], jnp.concatenate(rows, axis=0))
        for i, owner in enumerate(owners):
            found[owner] = result[:, CAP * i : CAP * (i + 1)]
            result_copy(owner, True)
        return carry

    lax.fori_loop(0, OWNERS // 2, pick, 0)

    def finish(i, carry):
        label_copy(i, False)
        for z in range(3):
            plane_copy(z, i, False)
        result_copy(i, False)
        arrive(out.at[i], out_recv.at[i])
        return carry

    lax.fori_loop(0, OWNERS, finish, 0)


def on_device(sticks, stick_columns):
    tables = [jnp.asarray(TABLES[name]) for name in STAGES]
    anywhere = pl.BlockSpec(memory_space=pl.ANY)
    dma = pltpu.SemaphoreType.DMA
    result = pl.pallas_call(
        exchange_kernel,
        out_shape=jax.ShapeDtypeStruct((OWNERS, 2 * G, CAP), F32),
        in_specs=[pl.BlockSpec(memory_space=pltpu.VMEM)] * 2 + [anywhere] * len(tables),
        out_specs=anywhere,
        scratch_shapes=[pltpu.VMEM(t.shape, t.dtype) for t in tables]
        + [
            pltpu.VMEM((OWNERS, 2 * G, CAP), F32),
            pltpu.VMEM((3, OWNERS, 32, CAP), F32),
            pltpu.VMEM((OWNERS, 1, CAP), jnp.int32),
            pltpu.VMEM((6 * G, 256), F32),
            pltpu.VMEM((5, 3, G, WIDE), F32),
            pltpu.VMEM((ROWS, WIDE), F32),
            pltpu.VMEM((WIDE, 12 * G), BF16),
            pltpu.VMEM((OWNERS, 2 * G, CAP), F32),
            dma((len(tables),)),
            dma((3, OWNERS)),
            dma((3, OWNERS)),
            dma((OWNERS,)),
            dma((OWNERS,)),
            dma((4, 3)),
            dma((5, 3)),
            dma((OWNERS,)),
            dma((OWNERS,)),
        ],
        compiler_params=pltpu.CompilerParams(collective_id=0, has_side_effects=True, vmem_limit_bytes=56 << 20),
    )(sticks, stick_columns.reshape(1, CAP), *tables)
    return result * np.float32(G**-1.5)


def solution(mesh):
    return jax.shard_map(
        on_device,
        mesh=mesh,
        in_specs=(P("band", None, "stick"), P("stick")),
        out_specs=P("band", None, "stick"),
        check_vma=False,
    )
```

```python
import functools
import math

import jax
import jax.numpy as jnp
import ml_dtypes
import numpy as np
from jax import lax
from jax.experimental import pallas as pl
from jax.experimental.pallas import tpu as pltpu
from jax.sharding import PartitionSpec as P

G = 48
ROWS, WIDE = 3 * G, 16 * G
OWNERS = 16
CAP = 128
BOX_LENGTH = 18.0
F32, BF16 = jnp.float32, jnp.bfloat16


def two_parts(table):
    high = table.astype(ml_dtypes.bfloat16)
    low = (table - high.astype(np.float64)).astype(ml_dtypes.bfloat16)
    return high, low


def stacked(table):
    high, low = two_parts(table)
    return np.concatenate([high, high, low], axis=1)


def make_tables():
    index = np.arange(G)
    angle = 2.0 * np.pi / G * (np.outer(index, index) % G)
    cos, sin = np.cos(angle), np.sin(angle)
    plus = (cos + sin) / np.sqrt(G)
    minus = (cos - sin) / np.sqrt(G)
    on_y = np.kron(plus, np.eye(16))
    on_z = np.einsum("aibj,kl->akiblj", plus.reshape(3, 16, 3, 16), np.eye(8)).reshape(384, 384)
    folded = np.minimum(index, G - index).astype(np.float64) ** 2
    total = folded[:, None, None] + folded[None, :, None] + folded[None, None, :]
    kernel = np.where(total > 0, 4.0 * np.pi / ((2.0 * np.pi / BOX_LENGTH) ** 2 * np.maximum(total, 1.0)), 0.0)
    kernel = kernel.reshape(G, 6, 8, 3, 16).transpose(3, 0, 1, 2, 4).reshape(ROWS, WIDE)
    z_in = np.block([[cos, -sin], [sin, cos]]).reshape(2, 3, 16, 2 * G).transpose(1, 0, 2, 3).reshape(2 * G, 2 * G)
    z_out = np.block([[cos, sin], [-sin, cos]])
    return dict(
        x=stacked(plus),
        x_in=stacked(np.concatenate([plus, minus], axis=1) * (0.5 * G)),
        x_out=stacked(np.concatenate([plus, minus], axis=0) * (0.5 * G)),
        y_high=two_parts(on_y)[0],
        y_low=two_parts(on_y)[1],
        z_high=two_parts(on_z)[0],
        z_low=two_parts(on_z)[1],
        kernel=kernel.astype(np.float32),
        z_in=stacked(z_in),
        z_out=stacked(z_out),
    )


TABLES = make_tables()


def dot(left, right):
    return jnp.dot(left, right, preferred_element_type=F32)


def split(value):
    high = value.astype(BF16)
    return high, (value - high.astype(F32)).astype(BF16)


def left_product(table, value):
    high, low = split(value)
    return dot(table, jnp.concatenate([high, low, high], axis=0))


def right_product(value, high_table, low_table):
    high, low = split(value)
    rows = value.shape[0]
    both = dot(jnp.concatenate([high, low], axis=0), high_table)
    return both[:rows] + both[rows:] + dot(high, low_table)


MESH = pl.DeviceIdType.MESH
STAGES = tuple(TABLES)


def chip_of(pair):
    place = (pair + 6) % 8
    row = place // 4
    return place + row * (7 - 2 * place), row


def computer_of(pair, core, member):
    x, row = chip_of(pair)
    return row * 8 + member % 8, x * 4 + member // 8 * 2 + core


def role_of(stick, band):
    row, x = stick // 8, band // 4
    place = x + row * (7 - 2 * x)
    return (place + 2) % 8, band % 2, band % 4 // 2 * 8 + stick % 8


def y_stage(field, high, low):
    return right_product(field, high, low)


def z_stage(field, high, low):
    starts = range(0, field.shape[0], ROWS)
    rows = [
        jnp.concatenate([field[a + G * z : a + G * (z + 1), 128 * y : 128 * (y + 1)] for z in range(3)], axis=1)
        for a in starts
        for y in range(6)
    ]
    out = right_product(jnp.concatenate(rows, axis=0), high, low)
    return jnp.concatenate(
        [
            jnp.concatenate([out[2 * a + G * y : 2 * a + G * (y + 1), 128 * z : 128 * (z + 1)] for y in range(6)], axis=1)
            for a in starts
            for z in range(3)
        ],
        axis=0,
    )


def x_stage(field, table):
    return jnp.concatenate([left_product(table, field[G * z : G * (z + 1)]) for z in range(field.shape[0] // G)], axis=0)


def reflected(tiles):
    lane = lax.broadcasted_iota(jnp.int32, (G, 128), 1) // 16
    out = []
    for y in range(6):
        source = tiles[5 - y]
        turned = jnp.where(
            lane == 4,
            source,
            jnp.where(
                lane % 4 == 1,
                pltpu.roll(source, 32, 1),
                jnp.where(lane % 4 == 2, pltpu.roll(source, 64, 1), pltpu.roll(source, 96, 1)),
            ),
        )
        out.append(jnp.where(lane == 0, tiles[(6 - y) % 6], turned))
    return out


def slot_places(columns):
    kx = (columns * 43691) >> 21
    ky = columns - kx * G
    row = (ky >> 3) * G + kx
    return jnp.where(columns >= 0, row, -1), ky & 7


def one_hot(row):
    places = lax.broadcasted_iota(jnp.int32, (6 * G, row.shape[1]), 0)
    return jnp.where(places == row, 1.0, 0.0).astype(BF16)


def exchange_kernel(sticks, labels, *refs):
    count = len(STAGES)
    stored, out, held = refs[:count], refs[count], refs[count + 1 : 2 * count + 1]
    t = dict(zip(STAGES, held))
    (given, sent, blocks, columns, grid, fields, total, turned, found, table_sem, in_send, in_recv, label_send, label_recv,
     field_send, field_recv, out_send, out_recv) = refs[2 * count + 1 :]
    stick, band = lax.axis_index("stick"), lax.axis_index("band")
    pair, core, member = role_of(stick, band)
    group = 2 * pair + core

    home = group == band
    own_row, own_column = computer_of(band // 2, band % 2, 0)

    def own_computer(i):
        return own_row + i % 8, own_column + i // 8 * 2

    upper, lower = (pair + 1) % 8, (pair + 7) % 8
    to_upper, to_lower = computer_of(upper, 0, member), computer_of(lower, 1, member)
    partner = computer_of(pair, 1 - core, member)
    beyond = core * upper + (1 - core) * lower
    from_first, from_second = computer_of(beyond, 0, member), computer_of(beyond, 1, member)

    barrier = pltpu.get_barrier_semaphore()

    def signal(device):
        pl.semaphore_signal(barrier, 1, device_id=device, device_id_type=MESH)

    def greet(i, carry):
        @pl.when(jnp.logical_not(jnp.logical_and(home, i == stick)))
        def _():
            signal((i, group))

        @pl.when(jnp.logical_not(jnp.logical_and(home, i == member)))
        def _():
            signal(own_computer(i))

        return carry

    lax.fori_loop(0, OWNERS, greet, 0)
    for device in (from_first, from_second, partner):
        signal(device)

    own_load = pltpu.make_async_copy(sticks, given, table_sem.at[count])
    own_load.start()
    loads = [pltpu.make_async_copy(a, b, table_sem.at[i]) for i, (a, b) in enumerate(zip(stored, held))]
    first_load = STAGES.index("z_in")
    loads[first_load].start()
    for i, load in enumerate(loads):
        if i != first_load:
            load.start()
    loads[first_load].wait()
    own_load.wait()

    def to_planes(i, carry):
        pair = jnp.concatenate([given[2 * i], given[2 * i + 1]], axis=1)
        pair = left_product(t["z_in"][...], pair)
        sent[2 * i] = pair[:, :CAP]
        sent[2 * i + 1] = pair[:, CAP:]
        return carry

    lax.fori_loop(0, OWNERS // 2, to_planes, 0)
    pl.semaphore_wait(barrier, 2 * OWNERS + 3 - 2 * jnp.where(home, 1, 0))

    def either(same, device, source, target, out_sem, in_sem, start):
        here = jnp.logical_and(home, same)
        if start:

            @pl.when(here)
            def _():
                pltpu.make_async_copy(source, target, in_sem).start()

        @pl.when(jnp.logical_not(here))
        def _():
            copy = pltpu.make_async_remote_copy(
                source, target, out_sem, in_sem, device_id=device, device_id_type=MESH
            )
            if start:
                copy.start()
            else:
                copy.wait_send()

    def label_copy(i, start):
        either(i == member, own_computer(i), labels, columns.at[stick], label_send.at[i], label_recv.at[stick], start)

    def plane_copy(z, i, start):
        source, target = sent.at[i, pl.ds(pl.multiple_of(32 * z, 32), 32)], blocks.at[z, stick]
        either(i == member, own_computer(i), source, target, in_send.at[z, i], in_recv.at[z, stick], start)

    def send_labels(step, carry):
        label_copy((stick + step) % OWNERS, True)
        return carry

    def send_planes(index, carry):
        plane_copy(index // OWNERS, (stick + index) % OWNERS, True)
        return carry

    lax.fori_loop(0, OWNERS, send_labels, 0)
    lax.fori_loop(0, 3 * OWNERS, send_planes, 0)

    spans = lax.broadcasted_iota(jnp.int32, (128, CAP), 0) >> 4

    def arrive(ref, sem):
        pltpu.make_async_copy(ref, ref, sem).wait()

    def field_copy(source, slot, z, index, device):
        return pltpu.make_async_remote_copy(
            fields.at[source, z],
            fields.at[slot, z],
            field_send.at[index, z],
            field_recv.at[slot, z],
            device_id=device,
            device_id_type=MESH,
        )

    def outward(z):
        return [
            field_copy(0, 2 + core, z, 0, to_upper),
            field_copy(0, 2 + core, z, 1, to_lower),
            field_copy(0, 1, z, 2, partner),
        ]

    def onward(z):
        return field_copy(3 - core, 4, z, 3, partner)

    def plane(z, carry):
        grid[...] = jnp.zeros_like(grid)

        def place(step, carry):
            owners = [(member + OWNERS - 4 * step - i) % OWNERS for i in range(4)]

            @pl.when(z == 0)
            def _():
                for owner in owners:
                    arrive(columns.at[owner], label_recv.at[owner])

            hots, spreads = [], []
            for owner in owners:
                arrive(blocks.at[z, owner], in_recv.at[z, owner])
            for owner in owners:
                row, span = slot_places(columns[owner])
                keep = jnp.where(spans == span, 1.0, 0.0).astype(BF16)
                for part in split(blocks[z, owner]):
                    parts = [jnp.concatenate([part[16 * i : 16 * i + 16]] * 8, axis=0) * keep for i in range(2)]
                    spreads.append(jnp.concatenate(parts, axis=0))
                hots += [one_hot(row)] * 2
            grid[...] += lax.dot_general(
                jnp.concatenate(hots, axis=1),
                jnp.concatenate(spreads, axis=1),
                (((1,), (1,)), ((), ())),
                preferred_element_type=F32,
            )
            return carry

        lax.fori_loop(0, OWNERS // 4, place, 0)

        @pl.when(z == 0)
        def _():
            for i, load in enumerate(loads):
                if i != first_load:
                    load.wait()

        @pl.when(z > 0)
        def _():
            arrive(fields.at[3 - core, z - 1], field_recv.at[3 - core, z - 1])
            onward(z - 1).start()

        real = [grid[G * y : G * (y + 1), :128] for y in range(6)]
        imag = [grid[G * y : G * (y + 1), 128:] for y in range(6)]
        first = jnp.concatenate([a - b for a, b in zip(reflected(real), imag)], axis=1)
        second = jnp.concatenate([a + b for a, b in zip(real, reflected(imag))], axis=1)
        both = y_stage(jnp.concatenate([first, second], axis=0), t["y_high"][...], t["y_low"][...])
        fields[0, z] = left_product(t["x_in"][...], both)
        for copy in outward(z):
            copy.start()

        return carry

    lax.fori_loop(0, 3, plane, 0)
    def arrive_field(slot):
        for z in range(3):
            arrive(fields.at[slot, z], field_recv.at[slot, z])

    def pots(slots):
        sources = [fields[slot].reshape(ROWS, WIDE) for slot in slots]
        own = fields[0].reshape(ROWS, WIDE)
        value = jnp.concatenate([own * source for source in sources], axis=0)
        value = x_stage(value, t["x"][...])
        value = y_stage(value, t["y_high"][...], t["y_low"][...])
        value = z_stage(value, t["z_high"][...], t["z_low"][...])
        value = value * jnp.concatenate([t["kernel"][...]] * len(slots), axis=0)
        value = z_stage(value, t["z_high"][...], t["z_low"][...])
        value = y_stage(value, t["y_high"][...], t["y_low"][...])
        value = x_stage(value, t["x"][...])
        return sum(value[ROWS * i : ROWS * (i + 1)] * source for i, source in enumerate(sources))

    arrive_field(1)
    total[...] = pots((0, 1))
    arrive(fields.at[3 - core, 2], field_recv.at[3 - core, 2])
    onward(2).start()
    arrive_field(2 + core)
    arrive_field(4)
    total[...] += pots((2, 3, 4))
    for z in range(3):
        for copy in outward(z):
            copy.wait_send()
        onward(z).wait_send()

    split_x = [left_product(t["x_out"][...], total[G * z : G * (z + 1), :]) for z in range(3)]
    both = y_stage(
        jnp.concatenate([v[:G] for v in split_x] + [v[G:] for v in split_x], axis=0), t["y_high"][...], t["y_low"][...]
    )

    def out_tiles(i):
        return [both[G * i : G * (i + 1), 128 * y : 128 * (y + 1)] for y in range(6)]

    real, imag = [], []
    for z in range(3):
        plus, minus = out_tiles(z), out_tiles(3 + z)
        real.append([a + b for a, b in zip(minus, reflected(plus))])
        imag.append([a - b for a, b in zip(reflected(minus), plus)])
    for i, part in enumerate(real + imag):
        high, low = split(jnp.concatenate(part, axis=0).T)
        turned[128 * i : 128 * (i + 1), : 6 * G] = high
        turned[128 * i : 128 * (i + 1), 6 * G :] = low

    def result_copy(owner, start):
        either(owner == stick, (owner, group), found.at[owner], out.at[member], out_send.at[owner], out_recv.at[member], start)

    def pick(step, carry):
        owners = [(member + OWNERS - 2 * step - i) % OWNERS for i in range(2)]
        row, span = slot_places(jnp.concatenate([columns[owner] for owner in owners], axis=1))
        hot = one_hot(row)
        picked = dot(turned[...], jnp.concatenate([hot, hot], axis=0))
        rows = []
        for i in range(6):
            value = jnp.zeros((16, 2 * CAP), F32)
            for g in range(8):
                start = 128 * i + 16 * g
                value = value + jnp.where(span == g, picked[start : start + 16], 0.0)
            rows.append(value)
        result = left_product(t["z_out"][...], jnp.concatenate(rows, axis=0))
        for i, owner in enumerate(owners):
            found[owner] = result[:, CAP * i : CAP * (i + 1)]
            result_copy(owner, True)
        return carry

    lax.fori_loop(0, OWNERS // 2, pick, 0)

    def finish(i, carry):
        label_copy(i, False)
        for z in range(3):
            plane_copy(z, i, False)
        result_copy(i, False)
        arrive(out.at[i], out_recv.at[i])
        return carry

    lax.fori_loop(0, OWNERS, finish, 0)


def on_device(sticks, stick_columns):
    tables = [jnp.asarray(TABLES[name]) for name in STAGES]
    anywhere = pl.BlockSpec(memory_space=pl.ANY)
    dma = pltpu.SemaphoreType.DMA
    result = pl.pallas_call(
        exchange_kernel,
        out_shape=jax.ShapeDtypeStruct((OWNERS, 2 * G, CAP), F32),
        in_specs=[anywhere] * (2 + len(tables)),
        out_specs=anywhere,
        scratch_shapes=[pltpu.VMEM(t.shape, t.dtype) for t in tables]
        + [
            pltpu.VMEM((OWNERS, 2 * G, CAP), F32),
            pltpu.VMEM((OWNERS, 2 * G, CAP), F32),
            pltpu.VMEM((3, OWNERS, 32, CAP), F32),
            pltpu.VMEM((OWNERS, 1, CAP), jnp.int32),
            pltpu.VMEM((6 * G, 256), F32),
            pltpu.VMEM((5, 3, G, WIDE), F32),
            pltpu.VMEM((ROWS, WIDE), F32),
            pltpu.VMEM((WIDE, 12 * G), BF16),
            pltpu.VMEM((OWNERS, 2 * G, CAP), F32),
            dma((len(tables) + 1,)),
            dma((3, OWNERS)),
            dma((3, OWNERS)),
            dma((OWNERS,)),
            dma((OWNERS,)),
            dma((4, 3)),
            dma((5, 3)),
            dma((OWNERS,)),
            dma((OWNERS,)),
        ],
        compiler_params=pltpu.CompilerParams(collective_id=0, has_side_effects=True, vmem_limit_bytes=56 << 20),
    )(sticks, stick_columns.reshape(1, CAP), *tables)
    return result * np.float32(G**-1.5)


def solution(mesh):
    return jax.shard_map(
        on_device,
        mesh=mesh,
        in_specs=(P("band", None, "stick"), P("stick")),
        out_specs=P("band", None, "stick"),
        check_vma=False,
    )
```

```python
import functools
import math

import jax
import jax.numpy as jnp
import ml_dtypes
import numpy as np
from jax import lax
from jax.experimental import pallas as pl
from jax.experimental.pallas import tpu as pltpu
from jax.sharding import PartitionSpec as P

G = 48
ROWS, WIDE = 3 * G, 16 * G
OWNERS = 16
CAP = 128
BOX_LENGTH = 18.0
F32, BF16 = jnp.float32, jnp.bfloat16


def two_parts(table):
    high = table.astype(ml_dtypes.bfloat16)
    low = (table - high.astype(np.float64)).astype(ml_dtypes.bfloat16)
    return high, low


def stacked(table):
    high, low = two_parts(table)
    return np.concatenate([high, high, low], axis=1)


def make_tables():
    index = np.arange(G)
    angle = 2.0 * np.pi / G * (np.outer(index, index) % G)
    cos, sin = np.cos(angle), np.sin(angle)
    plus = (cos + sin) / np.sqrt(G)
    minus = (cos - sin) / np.sqrt(G)
    on_y = np.kron(plus, np.eye(16))
    on_z = np.einsum("aibj,kl->akiblj", plus.reshape(3, 16, 3, 16), np.eye(8)).reshape(384, 384)
    folded = np.minimum(index, G - index).astype(np.float64) ** 2
    total = folded[:, None, None] + folded[None, :, None] + folded[None, None, :]
    kernel = np.where(total > 0, 4.0 * np.pi / ((2.0 * np.pi / BOX_LENGTH) ** 2 * np.maximum(total, 1.0)), 0.0)
    kernel = kernel.reshape(G, 6, 8, 3, 16).transpose(3, 0, 1, 2, 4).reshape(ROWS, WIDE)
    z_in = np.block([[cos, -sin], [sin, cos]]).reshape(2, 3, 16, 2 * G).transpose(1, 0, 2, 3).reshape(2 * G, 2 * G)
    z_out = np.block([[cos, sin], [-sin, cos]]).reshape(2 * G, 2, 3, 16).transpose(0, 2, 1, 3).reshape(2 * G, 2 * G)
    return dict(
        x=stacked(plus),
        x_in=stacked(np.concatenate([plus, minus], axis=1) * (0.5 * G)),
        x_out=stacked(np.concatenate([plus, minus], axis=0) * (0.5 * G)),
        y_high=two_parts(on_y)[0],
        y_low=two_parts(on_y)[1],
        z=stacked(on_z.T).T.copy(),
        kernel=kernel.astype(np.float32),
        z_in=stacked(z_in),
        z_out=stacked(z_out),
    )


TABLES = make_tables()


def dot(left, right):
    return jnp.dot(left, right, preferred_element_type=F32)


def split(value):
    high = value.astype(BF16)
    return high, (value - high.astype(F32)).astype(BF16)


def left_product(table, value):
    high, low = split(value)
    return dot(table, jnp.concatenate([high, low, high], axis=0))


def right_product(value, high_table, low_table):
    high, low = split(value)
    rows = value.shape[0]
    both = dot(jnp.concatenate([high, low], axis=0), high_table)
    return both[:rows] + both[rows:] + dot(high, low_table)


MESH = pl.DeviceIdType.MESH
STAGES = tuple(TABLES)


def chip_of(pair):
    place = (pair + 6) % 8
    row = place // 4
    return place + row * (7 - 2 * place), row


def computer_of(pair, core, member):
    x, row = chip_of(pair)
    return row * 8 + member % 8, x * 4 + member // 8 * 2 + core


def role_of(stick, band):
    row, x = stick // 8, band // 4
    place = x + row * (7 - 2 * x)
    return (place + 2) % 8, band % 2, band % 4 // 2 * 8 + stick % 8


def y_stage(field, high, low):
    return right_product(field, high, low)


def z_stage(field, table):
    starts = range(0, field.shape[0], ROWS)
    rows = [
        jnp.concatenate([field[a + G * z : a + G * (z + 1), 128 * y : 128 * (y + 1)] for z in range(3)], axis=1)
        for a in starts
        for y in range(6)
    ]
    high, low = split(jnp.concatenate(rows, axis=0))
    out = dot(jnp.concatenate([high, low, high], axis=1), table)
    return jnp.concatenate(
        [
            jnp.concatenate([out[2 * a + G * y : 2 * a + G * (y + 1), 128 * z : 128 * (z + 1)] for y in range(6)], axis=1)
            for a in starts
            for z in range(3)
        ],
        axis=0,
    )


def x_stage(field, table):
    return jnp.concatenate([left_product(table, field[G * z : G * (z + 1)]) for z in range(field.shape[0] // G)], axis=0)


def reflected(tiles):
    lane = lax.broadcasted_iota(jnp.int32, (G, 128), 1) // 16
    out = []
    for y in range(6):
        source = tiles[5 - y]
        turned = jnp.where(
            lane == 4,
            source,
            jnp.where(
                lane % 4 == 1,
                pltpu.roll(source, 32, 1),
                jnp.where(lane % 4 == 2, pltpu.roll(source, 64, 1), pltpu.roll(source, 96, 1)),
            ),
        )
        out.append(jnp.where(lane == 0, tiles[(6 - y) % 6], turned))
    return out


def slot_places(columns):
    kx = (columns * 43691) >> 21
    ky = columns - kx * G
    row = (ky >> 3) * G + kx
    return jnp.where(columns >= 0, row, -1), ky & 7


def one_hot(row):
    places = lax.broadcasted_iota(jnp.int32, (6 * G, row.shape[1]), 0)
    return jnp.where(places == row, 1.0, 0.0).astype(BF16)


def exchange_kernel(sticks, labels, *refs):
    count = len(STAGES)
    stored, out, held = refs[:count], refs[count], refs[count + 1 : 2 * count + 1]
    t = dict(zip(STAGES, held))
    (given, sent, blocks, columns, grid, fields, work, total, turned, found, back, ready, table_sem, in_send, in_recv,
     label_send, label_recv, field_send, field_recv, out_send, out_recv, out_store) = refs[2 * count + 1 :]
    stick, band = lax.axis_index("stick"), lax.axis_index("band")
    pair, core, member = role_of(stick, band)
    group = 2 * pair + core

    home = group == band
    own_row, own_column = computer_of(band // 2, band % 2, 0)

    def own_computer(i):
        return own_row + i % 8, own_column + i // 8 * 2

    upper, lower = (pair + 1) % 8, (pair + 7) % 8
    to_upper, to_lower = computer_of(upper, 0, member), computer_of(lower, 1, member)
    partner = computer_of(pair, 1 - core, member)
    beyond = core * upper + (1 - core) * lower
    from_first, from_second = computer_of(beyond, 0, member), computer_of(beyond, 1, member)

    barrier = pltpu.get_barrier_semaphore()

    def signal(device):
        pl.semaphore_signal(barrier, 1, device_id=device, device_id_type=MESH)

    def greet(i, carry):
        @pl.when(jnp.logical_not(jnp.logical_and(home, i == stick)))
        def _():
            signal((i, group))

        @pl.when(jnp.logical_not(jnp.logical_and(home, i == member)))
        def _():
            signal(own_computer(i))

        return carry

    lax.fori_loop(0, OWNERS, greet, 0)
    for device in (from_first, from_second, partner):
        signal(device)

    own_load = pltpu.make_async_copy(sticks, given, table_sem.at[count])
    own_load.start()
    loads = [pltpu.make_async_copy(a, b, table_sem.at[i]) for i, (a, b) in enumerate(zip(stored, held))]
    first_load = STAGES.index("z_in")
    loads[first_load].start()
    for i, load in enumerate(loads):
        if i != first_load:
            load.start()
    loads[first_load].wait()
    own_load.wait()

    def to_planes(i, carry):
        pair = jnp.concatenate([given[2 * i], given[2 * i + 1]], axis=1)
        pair = left_product(t["z_in"][...], pair)
        sent[2 * i] = pair[:, :CAP]
        sent[2 * i + 1] = pair[:, CAP:]
        return carry

    lax.fori_loop(0, OWNERS // 2, to_planes, 0)
    pl.semaphore_wait(barrier, 2 * OWNERS + 3 - 2 * jnp.where(home, 1, 0))

    def either(same, device, source, target, out_sem, in_sem, start):
        here = jnp.logical_and(home, same)
        if start:

            @pl.when(here)
            def _():
                pltpu.make_async_copy(source, target, in_sem).start()

        @pl.when(jnp.logical_not(here))
        def _():
            copy = pltpu.make_async_remote_copy(
                source, target, out_sem, in_sem, device_id=device, device_id_type=MESH
            )
            if start:
                copy.start()
            else:
                copy.wait_send()

    def label_copy(i, start):
        either(i == member, own_computer(i), labels, columns.at[stick], label_send.at[i], label_recv.at[stick], start)

    def plane_copy(z, i, start):
        source, target = sent.at[i, pl.ds(pl.multiple_of(32 * z, 32), 32)], blocks.at[z, stick]
        either(i == member, own_computer(i), source, target, in_send.at[z, i], in_recv.at[z, stick], start)

    def send_labels(step, carry):
        label_copy((stick + step) % OWNERS, True)
        return carry

    def send_planes(index, carry):
        plane_copy(index // OWNERS, (stick + index) % OWNERS, True)
        return carry

    lax.fori_loop(0, OWNERS, send_labels, 0)
    lax.fori_loop(0, 3 * OWNERS, send_planes, 0)

    spans = lax.broadcasted_iota(jnp.int32, (128, CAP), 0) >> 4

    def arrive(ref, sem):
        pltpu.make_async_copy(ref, ref, sem).wait()

    def field_copy(source, slot, z, index, device):
        return pltpu.make_async_remote_copy(
            fields.at[source, z],
            fields.at[slot, z],
            field_send.at[index, z],
            field_recv.at[slot, z],
            device_id=device,
            device_id_type=MESH,
        )

    def outward(z):
        return [
            field_copy(0, 2 + core, z, 0, to_upper),
            field_copy(0, 2 + core, z, 1, to_lower),
            field_copy(0, 1, z, 2, partner),
        ]

    def onward(z):
        return field_copy(3 - core, 4, z, 3, partner)

    def pass_on(z):
        arrive(fields.at[3 - core, z], field_recv.at[3 - core, z])
        onward(z).start()

    def plane(z, carry):
        grid[...] = jnp.zeros_like(grid)

        def place(step, carry):
            owners = [(member + OWNERS - 4 * step - i) % OWNERS for i in range(4)]

            @pl.when(z == 0)
            def _():
                for owner in owners:
                    arrive(columns.at[owner], label_recv.at[owner])

            hots, spreads = [], []
            for owner in owners:
                arrive(blocks.at[z, owner], in_recv.at[z, owner])
            for owner in owners:
                row, span = slot_places(columns[owner])
                keep = jnp.where(spans == span, 1.0, 0.0).astype(BF16)
                for part in split(blocks[z, owner]):
                    parts = [jnp.concatenate([part[16 * i : 16 * i + 16]] * 8, axis=0) * keep for i in range(2)]
                    spreads.append(jnp.concatenate(parts, axis=0))
                hots += [one_hot(row)] * 2
            grid[...] += lax.dot_general(
                jnp.concatenate(hots, axis=1),
                jnp.concatenate(spreads, axis=1),
                (((1,), (1,)), ((), ())),
                preferred_element_type=F32,
            )
            return carry

        lax.fori_loop(0, OWNERS // 4, place, 0)

        @pl.when(z == 0)
        def _():
            for i, load in enumerate(loads):
                if i != first_load:
                    load.wait()

        @pl.when(z == 2)
        def _():
            pass_on(0)

        real = [grid[G * y : G * (y + 1), :128] for y in range(6)]
        imag = [grid[G * y : G * (y + 1), 128:] for y in range(6)]
        first = jnp.concatenate([a - b for a, b in zip(reflected(real), imag)], axis=1)
        second = jnp.concatenate([a + b for a, b in zip(real, reflected(imag))], axis=1)
        both = y_stage(jnp.concatenate([first, second], axis=0), t["y_high"][...], t["y_low"][...])
        fields[0, z] = left_product(t["x_in"][...], both)
        for copy in outward(z):
            copy.start()

        return carry

    lax.fori_loop(0, 3, plane, 0)
    pass_on(1)

    own = fields[0].reshape(ROWS, WIDE)
    value = x_stage(own * own, t["x"][...])
    value = y_stage(value, t["y_high"][...], t["y_low"][...])
    value = z_stage(value, t["z"][...]) * t["kernel"][...]
    value = y_stage(z_stage(value, t["z"][...]), t["y_high"][...], t["y_low"][...])
    total[...] = (x_stage(value, t["x"][...]) * own).reshape(3, G, WIDE)

    def forward(z, carry):
        @pl.when(z == 1)
        def _():
            pass_on(2)

        arrive(fields.at[1, z], field_recv.at[1, z])
        arrive(fields.at[2 + core, z], field_recv.at[2 + core, z])
        arrive(fields.at[4, z], field_recv.at[4, z])
        value = jnp.concatenate([fields[0, z] * fields[slot, z] for slot in range(1, 5)], axis=0)
        value = y_stage(x_stage(value, t["x"][...]), t["y_high"][...], t["y_low"][...])
        for i in range(4):
            work[i, z] = value[G * i : G * (i + 1)]
        return carry

    lax.fori_loop(0, 3, forward, 0)
    value = z_stage(work[...].reshape(4 * ROWS, WIDE), t["z"][...])
    value = value * jnp.concatenate([t["kernel"][...]] * 4, axis=0)
    work[...] = z_stage(value, t["z"][...]).reshape(4, 3, G, WIDE)

    def result_copy(z, owner, start):
        device = (owner, group)
        source, target = found.at[z, owner], back.at[member, z]
        either(owner == stick, device, source, target, out_send.at[z, owner], out_recv.at[member, z], start)

    def backward(z, carry):
        value = jnp.concatenate([work[i, z] for i in range(4)], axis=0)
        value = x_stage(y_stage(value, t["y_high"][...], t["y_low"][...]), t["x"][...])
        field = total[z]
        for i in range(4):
            field = field + value[G * i : G * (i + 1)] * fields[i + 1, z]
        both = y_stage(left_product(t["x_out"][...], field), t["y_high"][...], t["y_low"][...])
        plus, minus = [[both[a : a + G, 128 * y : 128 * (y + 1)] for y in range(6)] for a in (0, G)]
        real = [a + b for a, b in zip(minus, reflected(plus))]
        imag = [a - b for a, b in zip(reflected(minus), plus)]
        for i, part in enumerate((real, imag)):
            high, low = split(jnp.concatenate(part, axis=0).T)
            turned[128 * i : 128 * (i + 1), : 6 * G] = high
            turned[128 * i : 128 * (i + 1), 6 * G :] = low

        def pick(step, carry):
            owners = [(member + OWNERS - 2 * step - i) % OWNERS for i in range(2)]
            row, span = slot_places(jnp.concatenate([columns[owner] for owner in owners], axis=1))
            hot = one_hot(row)
            picked = dot(turned[...], jnp.concatenate([hot, hot], axis=0))
            rows = []
            for i in range(2):
                value = jnp.zeros((16, 2 * CAP), F32)
                for g in range(8):
                    start = 128 * i + 16 * g
                    value = value + jnp.where(span == g, picked[start : start + 16], 0.0)
                rows.append(value)
            result = jnp.concatenate(rows, axis=0)
            for i, owner in enumerate(owners):
                found[z, owner] = result[:, CAP * i : CAP * (i + 1)]
                result_copy(z, owner, True)
            return carry

        lax.fori_loop(0, OWNERS // 2, pick, 0)
        return carry

    lax.fori_loop(0, 3, backward, 0)

    def from_planes(step, carry):
        bands = [(stick + 2 * step + i) % OWNERS for i in range(2)]
        for band_index in bands:
            for z in range(3):
                arrive(back.at[band_index, z], out_recv.at[band_index, z])
        pair = jnp.concatenate([back[band_index].reshape(2 * G, CAP) for band_index in bands], axis=1)
        pair = left_product(t["z_out"][...], pair)
        for i, band_index in enumerate(bands):
            ready[band_index] = pair[:, CAP * i : CAP * (i + 1)]
            pltpu.make_async_copy(ready.at[band_index], out.at[band_index], out_store.at[band_index]).start()
        return carry

    lax.fori_loop(0, OWNERS // 2, from_planes, 0)
    for z in range(3):
        for copy in outward(z):
            copy.wait_send()
        onward(z).wait_send()

    def finish(i, carry):
        label_copy(i, False)
        for z in range(3):
            plane_copy(z, i, False)
            result_copy(z, i, False)
        pltpu.make_async_copy(ready.at[i], out.at[i], out_store.at[i]).wait()
        return carry

    lax.fori_loop(0, OWNERS, finish, 0)


def on_device(sticks, stick_columns):
    tables = [jnp.asarray(TABLES[name]) for name in STAGES]
    anywhere, hbm = pl.BlockSpec(memory_space=pl.ANY), pl.BlockSpec(memory_space=pltpu.HBM)
    dma = pltpu.SemaphoreType.DMA
    result = pl.pallas_call(
        exchange_kernel,
        out_shape=jax.ShapeDtypeStruct((OWNERS, 2 * G, CAP), F32),
        in_specs=[hbm] * (2 + len(tables)),
        out_specs=anywhere,
        scratch_shapes=[pltpu.VMEM(t.shape, t.dtype) for t in tables]
        + [
            pltpu.VMEM((OWNERS, 2 * G, CAP), F32),
            pltpu.VMEM((OWNERS, 2 * G, CAP), F32),
            pltpu.VMEM((3, OWNERS, 32, CAP), F32),
            pltpu.VMEM((OWNERS, 1, CAP), jnp.int32),
            pltpu.VMEM((6 * G, 256), F32),
            pltpu.VMEM((5, 3, G, WIDE), F32),
            pltpu.VMEM((4, 3, G, WIDE), F32),
            pltpu.VMEM((3, G, WIDE), F32),
            pltpu.VMEM((256, 12 * G), BF16),
            pltpu.VMEM((3, OWNERS, 32, CAP), F32),
            pltpu.VMEM((OWNERS, 3, 32, CAP), F32),
            pltpu.VMEM((OWNERS, 2 * G, CAP), F32),
            dma((len(tables) + 1,)),
            dma((3, OWNERS)),
            dma((3, OWNERS)),
            dma((OWNERS,)),
            dma((OWNERS,)),
            dma((4, 3)),
            dma((5, 3)),
            dma((3, OWNERS)),
            dma((OWNERS, 3)),
            dma((OWNERS,)),
        ],
        compiler_params=pltpu.CompilerParams(collective_id=0, has_side_effects=True, vmem_limit_bytes=56 << 20),
    )(sticks, stick_columns.reshape(1, CAP), *tables)
    return result * np.float32(G**-1.5)


def solution(mesh):
    return jax.shard_map(
        on_device,
        mesh=mesh,
        in_specs=(P("band", None, "stick"), P("stick")),
        out_specs=P("band", None, "stick"),
        check_vma=False,
    )
```

```python
import functools
import math

import jax
import jax.numpy as jnp
import ml_dtypes
import numpy as np
from jax import lax
from jax.experimental import pallas as pl
from jax.experimental.pallas import tpu as pltpu
from jax.sharding import PartitionSpec as P

G = 48
ROWS, WIDE = 3 * G, 16 * G
OWNERS = 16
CAP = 128
BOX_LENGTH = 18.0
F32, BF16 = jnp.float32, jnp.bfloat16


def two_parts(table):
    high = table.astype(ml_dtypes.bfloat16)
    low = (table - high.astype(np.float64)).astype(ml_dtypes.bfloat16)
    return high, low


def stacked(table):
    high, low = two_parts(table)
    return np.concatenate([high, high, low], axis=1)


def make_tables():
    index = np.arange(G)
    angle = 2.0 * np.pi / G * (np.outer(index, index) % G)
    cos, sin = np.cos(angle), np.sin(angle)
    plus = (cos + sin) / np.sqrt(G)
    minus = (cos - sin) / np.sqrt(G)
    on_y = np.kron(plus, np.eye(16))
    on_z = np.einsum("aibj,kl->akiblj", plus.reshape(3, 16, 3, 16), np.eye(8)).reshape(384, 384)
    folded = np.minimum(index, G - index).astype(np.float64) ** 2
    total = folded[:, None, None] + folded[None, :, None] + folded[None, None, :]
    kernel = np.where(total > 0, 4.0 * np.pi / ((2.0 * np.pi / BOX_LENGTH) ** 2 * np.maximum(total, 1.0)), 0.0)
    kernel = kernel.reshape(G, 6, 8, 3, 16).transpose(3, 0, 1, 2, 4).reshape(ROWS, WIDE)
    z_in = np.block([[cos, -sin], [sin, cos]]).reshape(2, 3, 16, 2 * G).transpose(1, 0, 2, 3).reshape(2 * G, 2 * G)
    z_out = np.block([[cos, sin], [-sin, cos]]).reshape(2 * G, 2, 3, 16).transpose(0, 2, 1, 3).reshape(2 * G, 2 * G)
    return dict(
        x=stacked(plus),
        x_in=stacked(np.concatenate([plus, minus], axis=1) * (0.5 * G)),
        x_out=stacked(np.concatenate([plus, minus], axis=0) * (0.5 * G)),
        y_high=two_parts(on_y)[0],
        y_low=two_parts(on_y)[1],
        z=stacked(on_z.T).T.copy(),
        kernel=kernel.astype(np.float32),
        z_in=stacked(z_in),
        z_out=stacked(z_out),
    )


TABLES = make_tables()


def dot(left, right):
    return jnp.dot(left, right, preferred_element_type=F32)


def split(value):
    high = value.astype(BF16)
    return high, (value - high.astype(F32)).astype(BF16)


def left_product(table, value):
    high, low = split(value)
    return dot(table, jnp.concatenate([high, low, high], axis=0))


def right_product(value, high_table, low_table):
    high, low = split(value)
    rows = value.shape[0]
    both = dot(jnp.concatenate([high, low], axis=0), high_table)
    return both[:rows] + both[rows:] + dot(high, low_table)


MESH = pl.DeviceIdType.MESH
STAGES = tuple(TABLES)


def chip_of(pair):
    place = (pair + 6) % 8
    row = place // 4
    return place + row * (7 - 2 * place), row


def computer_of(pair, core, member):
    x, row = chip_of(pair)
    return row * 8 + member % 8, x * 4 + member // 8 * 2 + core


def role_of(stick, band):
    row, x = stick // 8, band // 4
    place = x + row * (7 - 2 * x)
    return (place + 2) % 8, band % 2, band % 4 // 2 * 8 + stick % 8


def y_stage(field, high, low):
    return right_product(field, high, low)


def z_stage(field, table):
    starts = range(0, field.shape[0], ROWS)
    rows = [
        jnp.concatenate([field[a + G * z : a + G * (z + 1), 128 * y : 128 * (y + 1)] for z in range(3)], axis=1)
        for a in starts
        for y in range(6)
    ]
    high, low = split(jnp.concatenate(rows, axis=0))
    out = dot(jnp.concatenate([high, low, high], axis=1), table)
    return jnp.concatenate(
        [
            jnp.concatenate([out[2 * a + G * y : 2 * a + G * (y + 1), 128 * z : 128 * (z + 1)] for y in range(6)], axis=1)
            for a in starts
            for z in range(3)
        ],
        axis=0,
    )


def x_stage(field, table):
    return jnp.concatenate([left_product(table, field[G * z : G * (z + 1)]) for z in range(field.shape[0] // G)], axis=0)


def reflected(tiles):
    lane = lax.broadcasted_iota(jnp.int32, (G, 128), 1) // 16
    out = []
    for y in range(6):
        source = tiles[5 - y]
        turned = jnp.where(
            lane == 4,
            source,
            jnp.where(
                lane % 4 == 1,
                pltpu.roll(source, 32, 1),
                jnp.where(lane % 4 == 2, pltpu.roll(source, 64, 1), pltpu.roll(source, 96, 1)),
            ),
        )
        out.append(jnp.where(lane == 0, tiles[(6 - y) % 6], turned))
    return out


def slot_places(columns):
    kx = (columns * 43691) >> 21
    ky = columns - kx * G
    row = (ky >> 3) * G + kx
    return jnp.where(columns >= 0, row, -1), ky & 7


def one_hot(row):
    places = lax.broadcasted_iota(jnp.int32, (6 * G, row.shape[1]), 0)
    return jnp.where(places == row, 1.0, 0.0).astype(BF16)


def exchange_kernel(sticks, labels, *refs):
    count = len(STAGES)
    stored, out, held = refs[:count], refs[count], refs[count + 1 : 2 * count + 1]
    t = dict(zip(STAGES, held))
    (given, sent, blocks, columns, grid, fields, work, total, turned, found, back, ready, table_sem, in_send, in_recv,
     label_send, label_recv, field_send, field_recv, out_send, out_recv, out_store) = refs[2 * count + 1 :]
    stick, band = lax.axis_index("stick"), lax.axis_index("band")
    pair, core, member = role_of(stick, band)
    group = 2 * pair + core

    home = group == band
    own_row, own_column = computer_of(band // 2, band % 2, 0)

    def own_computer(i):
        return own_row + i % 8, own_column + i // 8 * 2

    upper, lower = (pair + 1) % 8, (pair + 7) % 8
    to_upper, to_lower = computer_of(upper, 0, member), computer_of(lower, 1, member)
    partner = computer_of(pair, 1 - core, member)
    beyond = core * upper + (1 - core) * lower
    from_first, from_second = computer_of(beyond, 0, member), computer_of(beyond, 1, member)

    barrier = pltpu.get_barrier_semaphore()

    def signal(device):
        pl.semaphore_signal(barrier, 1, device_id=device, device_id_type=MESH)

    def greet(i, carry):
        @pl.when(jnp.logical_not(jnp.logical_and(home, i == stick)))
        def _():
            signal((i, group))

        @pl.when(jnp.logical_not(jnp.logical_and(home, i == member)))
        def _():
            signal(own_computer(i))

        return carry

    lax.fori_loop(0, OWNERS, greet, 0)
    for device in (from_first, from_second, partner):
        signal(device)

    own_load = pltpu.make_async_copy(sticks, given, table_sem.at[count])
    own_load.start()
    loads = [pltpu.make_async_copy(a, b, table_sem.at[i]) for i, (a, b) in enumerate(zip(stored, held))]
    first_load = STAGES.index("z_in")
    loads[first_load].start()
    for i, load in enumerate(loads):
        if i != first_load:
            load.start()
    loads[first_load].wait()
    own_load.wait()

    pl.semaphore_wait(barrier, 2 * OWNERS + 3 - 2 * jnp.where(home, 1, 0))

    def either(same, device, source, target, out_sem, in_sem):
        here = jnp.logical_and(home, same)

        @pl.when(here)
        def _():
            pltpu.make_async_copy(source, target, in_sem).start()

        @pl.when(jnp.logical_not(here))
        def _():
            pltpu.make_async_remote_copy(
                source, target, out_sem, in_sem, device_id=device, device_id_type=MESH
            ).start()

    def label_copy(i):
        batch = (i + OWNERS - stick) % OWNERS // 4
        either(i == member, own_computer(i), labels, columns.at[stick], label_send.at[0], label_recv.at[batch])

    def plane_copy(z, i):
        batch = (i + OWNERS - stick) % OWNERS // 4
        source, target = sent.at[i, pl.ds(pl.multiple_of(32 * z, 32), 32)], blocks.at[z, stick]
        either(i == member, own_computer(i), source, target, in_send.at[0], in_recv.at[z, batch])

    def to_planes(step, carry):
        bands = [(stick + 2 * step + i) % OWNERS for i in range(2)]
        pair = jnp.concatenate([given[i] for i in bands], axis=1)
        pair = left_product(t["z_in"][...], pair)
        for i, band_index in enumerate(bands):
            sent[band_index] = pair[:, CAP * i : CAP * (i + 1)]
            label_copy(band_index)
            plane_copy(0, band_index)
        return carry

    def send_planes(index, carry):
        plane_copy(index // OWNERS, (stick + index) % OWNERS)
        return carry

    lax.fori_loop(0, OWNERS // 2, to_planes, 0)
    lax.fori_loop(OWNERS, 3 * OWNERS, send_planes, 0)

    spans = lax.broadcasted_iota(jnp.int32, (128, CAP), 0) >> 4

    def arrive(ref, sem):
        pltpu.make_async_copy(ref, ref, sem).wait()

    def field_copy(source, slot, z, device):
        return pltpu.make_async_remote_copy(
            fields.at[source, z],
            fields.at[slot, z],
            field_send.at[0],
            field_recv.at[slot - 1, z],
            device_id=device,
            device_id_type=MESH,
        )

    def outward(z):
        return [
            field_copy(0, 2 + core, z, to_upper),
            field_copy(0, 2 + core, z, to_lower),
            field_copy(0, 1, z, partner),
        ]

    def onward(z):
        return field_copy(3 - core, 4, z, partner)

    def pass_on(z):
        arrive(fields.at[3 - core, z], field_recv.at[2 - core, z])
        onward(z).start()

    def plane(z, carry):
        grid[...] = jnp.zeros_like(grid)

        def place(step, carry):
            owners = [(member + OWNERS - 4 * step - i) % OWNERS for i in range(4)]

            @pl.when(z == 0)
            def _():
                arrive(columns.at[pl.ds(0, 4)], label_recv.at[step])

            hots, spreads = [], []
            arrive(blocks.at[z, pl.ds(0, 4)], in_recv.at[z, step])
            for owner in owners:
                row, span = slot_places(columns[owner])
                keep = jnp.where(spans == span, 1.0, 0.0).astype(BF16)
                for part in split(blocks[z, owner]):
                    parts = [jnp.concatenate([part[16 * i : 16 * i + 16]] * 8, axis=0) * keep for i in range(2)]
                    spreads.append(jnp.concatenate(parts, axis=0))
                hots += [one_hot(row)] * 2
            grid[...] += lax.dot_general(
                jnp.concatenate(hots, axis=1),
                jnp.concatenate(spreads, axis=1),
                (((1,), (1,)), ((), ())),
                preferred_element_type=F32,
            )
            return carry

        lax.fori_loop(0, OWNERS // 4, place, 0)

        @pl.when(z == 0)
        def _():
            for i, load in enumerate(loads):
                if i != first_load:
                    load.wait()

        @pl.when(z == 2)
        def _():
            pass_on(0)

        real = [grid[G * y : G * (y + 1), :128] for y in range(6)]
        imag = [grid[G * y : G * (y + 1), 128:] for y in range(6)]
        first = jnp.concatenate([a - b for a, b in zip(reflected(real), imag)], axis=1)
        second = jnp.concatenate([a + b for a, b in zip(real, reflected(imag))], axis=1)
        both = y_stage(jnp.concatenate([first, second], axis=0), t["y_high"][...], t["y_low"][...])
        fields[0, z] = left_product(t["x_in"][...], both)
        for copy in outward(z):
            copy.start()

        return carry

    lax.fori_loop(0, 3, plane, 0)
    pass_on(1)

    own = fields[0].reshape(ROWS, WIDE)
    value = x_stage(own * own, t["x"][...])
    value = y_stage(value, t["y_high"][...], t["y_low"][...])
    value = z_stage(value, t["z"][...]) * t["kernel"][...]
    value = y_stage(z_stage(value, t["z"][...]), t["y_high"][...], t["y_low"][...])
    total[...] = (x_stage(value, t["x"][...]) * own).reshape(3, G, WIDE)

    def forward(z, carry):
        @pl.when(z == 1)
        def _():
            pass_on(2)

        arrive(fields.at[1, z], field_recv.at[0, z])
        arrive(fields.at[2 + core, z], field_recv.at[1 + core, z])
        arrive(fields.at[4, z], field_recv.at[3, z])
        value = jnp.concatenate([fields[0, z] * fields[slot, z] for slot in range(1, 5)], axis=0)
        value = y_stage(x_stage(value, t["x"][...]), t["y_high"][...], t["y_low"][...])
        for i in range(4):
            work[i, z] = value[G * i : G * (i + 1)]
        return carry

    lax.fori_loop(0, 3, forward, 0)
    value = z_stage(work[...].reshape(4 * ROWS, WIDE), t["z"][...])
    value = value * jnp.concatenate([t["kernel"][...]] * 4, axis=0)
    work[...] = z_stage(value, t["z"][...]).reshape(4, 3, G, WIDE)

    def result_copy(z, owner):
        batch = (member + OWNERS - owner) % OWNERS // 2
        source, target = found.at[z, owner], back.at[member, z]
        either(owner == stick, (owner, group), source, target, out_send.at[0], out_recv.at[batch])

    def backward(z, carry):
        value = jnp.concatenate([work[i, z] for i in range(4)], axis=0)
        value = x_stage(y_stage(value, t["y_high"][...], t["y_low"][...]), t["x"][...])
        field = total[z]
        for i in range(4):
            field = field + value[G * i : G * (i + 1)] * fields[i + 1, z]
        both = y_stage(left_product(t["x_out"][...], field), t["y_high"][...], t["y_low"][...])
        plus, minus = [[both[a : a + G, 128 * y : 128 * (y + 1)] for y in range(6)] for a in (0, G)]
        real = [a + b for a, b in zip(minus, reflected(plus))]
        imag = [a - b for a, b in zip(reflected(minus), plus)]
        for i, part in enumerate((real, imag)):
            high, low = split(jnp.concatenate(part, axis=0).T)
            turned[128 * i : 128 * (i + 1), : 6 * G] = high
            turned[128 * i : 128 * (i + 1), 6 * G :] = low

        def pick(step, carry):
            owners = [(member + OWNERS - 2 * step - i) % OWNERS for i in range(2)]
            row, span = slot_places(jnp.concatenate([columns[owner] for owner in owners], axis=1))
            hot = one_hot(row)
            picked = dot(turned[...], jnp.concatenate([hot, hot], axis=0))
            rows = []
            for i in range(2):
                value = jnp.zeros((16, 2 * CAP), F32)
                for g in range(8):
                    start = 128 * i + 16 * g
                    value = value + jnp.where(span == g, picked[start : start + 16], 0.0)
                rows.append(value)
            result = jnp.concatenate(rows, axis=0)
            for i, owner in enumerate(owners):
                found[z, owner] = result[:, CAP * i : CAP * (i + 1)]
                result_copy(z, owner)
            return carry

        lax.fori_loop(0, OWNERS // 2, pick, 0)
        return carry

    lax.fori_loop(0, 3, backward, 0)

    def from_planes(step, carry):
        bands = [(stick + 2 * step + i) % OWNERS for i in range(2)]
        arrive(back.at[pl.ds(0, 2)], out_recv.at[step])
        pair = jnp.concatenate([back[band_index].reshape(2 * G, CAP) for band_index in bands], axis=1)
        pair = left_product(t["z_out"][...], pair)
        for i, band_index in enumerate(bands):
            ready[band_index] = pair[:, CAP * i : CAP * (i + 1)]
            pltpu.make_async_copy(ready.at[band_index], out.at[band_index], out_store.at[0]).start()
        return carry

    lax.fori_loop(0, OWNERS // 2, from_planes, 0)
    arrive(fields.at[pl.ds(0, 4)], field_send.at[0])

    @pl.when(home)
    def _():
        arrive(sent.at[pl.ds(0, OWNERS - 1)], in_send.at[0])
        arrive(columns.at[pl.ds(0, OWNERS - 1)], label_send.at[0])
        arrive(found.at[:, pl.ds(0, OWNERS - 1)], out_send.at[0])

    @pl.when(jnp.logical_not(home))
    def _():
        arrive(sent, in_send.at[0])
        arrive(columns, label_send.at[0])
        arrive(found, out_send.at[0])

    pltpu.make_async_copy(ready, out, out_store.at[0]).wait()


def on_device(sticks, stick_columns):
    tables = [jnp.asarray(TABLES[name]) for name in STAGES]
    anywhere, hbm = pl.BlockSpec(memory_space=pl.ANY), pl.BlockSpec(memory_space=pltpu.HBM)
    dma = pltpu.SemaphoreType.DMA
    result = pl.pallas_call(
        exchange_kernel,
        out_shape=jax.ShapeDtypeStruct((OWNERS, 2 * G, CAP), F32),
        in_specs=[hbm] * (2 + len(tables)),
        out_specs=anywhere,
        scratch_shapes=[pltpu.VMEM(t.shape, t.dtype) for t in tables]
        + [
            pltpu.VMEM((OWNERS, 2 * G, CAP), F32),
            pltpu.VMEM((OWNERS, 2 * G, CAP), F32),
            pltpu.VMEM((3, OWNERS, 32, CAP), F32),
            pltpu.VMEM((OWNERS, 1, CAP), jnp.int32),
            pltpu.VMEM((6 * G, 256), F32),
            pltpu.VMEM((5, 3, G, WIDE), F32),
            pltpu.VMEM((4, 3, G, WIDE), F32),
            pltpu.VMEM((3, G, WIDE), F32),
            pltpu.VMEM((256, 12 * G), BF16),
            pltpu.VMEM((3, OWNERS, 32, CAP), F32),
            pltpu.VMEM((OWNERS, 3, 32, CAP), F32),
            pltpu.VMEM((OWNERS, 2 * G, CAP), F32),
            dma((len(tables) + 1,)),
            dma((1,)),
            dma((3, 4)),
            dma((1,)),
            dma((4,)),
            dma((1,)),
            dma((4, 3)),
            dma((1,)),
            dma((OWNERS // 2,)),
            dma((1,)),
        ],
        compiler_params=pltpu.CompilerParams(collective_id=0, has_side_effects=True, vmem_limit_bytes=56 << 20),
    )(sticks, stick_columns.reshape(1, CAP), *tables)
    return result * np.float32(G**-1.5)


def solution(mesh):
    return jax.shard_map(
        on_device,
        mesh=mesh,
        in_specs=(P("band", None, "stick"), P("stick")),
        out_specs=P("band", None, "stick"),
        check_vma=False,
    )
```

```python
import functools
import math

import jax
import jax.numpy as jnp
import ml_dtypes
import numpy as np
from jax import lax
from jax.experimental import pallas as pl
from jax.experimental.pallas import tpu as pltpu
from jax.sharding import PartitionSpec as P

G = 48
ROWS, WIDE = 3 * G, 16 * G
OWNERS = 16
CAP = 128
BOX_LENGTH = 18.0
F32, BF16 = jnp.float32, jnp.bfloat16


def two_parts(table):
    high = table.astype(ml_dtypes.bfloat16)
    low = (table - high.astype(np.float64)).astype(ml_dtypes.bfloat16)
    return high, low


def stacked(table):
    high, low = two_parts(table)
    return np.concatenate([high, high, low], axis=1)


def make_tables():
    index = np.arange(G)
    angle = 2.0 * np.pi / G * (np.outer(index, index) % G)
    cos, sin = np.cos(angle), np.sin(angle)
    plus = (cos + sin) / np.sqrt(G)
    minus = (cos - sin) / np.sqrt(G)
    on_y = np.kron(plus, np.eye(16))
    on_z = np.einsum("aibj,kl->akiblj", plus.reshape(3, 16, 3, 16), np.eye(8)).reshape(384, 384)
    folded = np.minimum(index, G - index).astype(np.float64) ** 2
    total = folded[:, None, None] + folded[None, :, None] + folded[None, None, :]
    kernel = np.where(total > 0, 4.0 * np.pi / ((2.0 * np.pi / BOX_LENGTH) ** 2 * np.maximum(total, 1.0)), 0.0)
    kernel = kernel.reshape(G, 6, 8, 3, 16).transpose(3, 0, 1, 2, 4).reshape(ROWS, WIDE)
    z_in = np.block([[cos, -sin], [sin, cos]]).reshape(2, 3, 16, 2 * G).transpose(1, 0, 2, 3).reshape(2 * G, 2 * G)
    z_out = np.block([[cos, sin], [-sin, cos]]).reshape(2 * G, 2, 3, 16).transpose(0, 2, 1, 3).reshape(2 * G, 2 * G)
    return dict(
        x=stacked(plus),
        x_in=stacked(np.concatenate([plus, minus], axis=1) * (0.5 * G)),
        x_out=stacked(np.concatenate([plus, minus], axis=0) * (0.5 * G)),
        y_high=two_parts(on_y)[0],
        y_low=two_parts(on_y)[1],
        z=stacked(on_z.T).T.copy(),
        kernel=kernel.astype(np.float32),
        z_in=stacked(z_in),
        z_out=stacked(z_out),
    )


TABLES = make_tables()


def dot(left, right):
    return jnp.dot(left, right, preferred_element_type=F32)


def split(value):
    high = value.astype(BF16)
    return high, (value - high.astype(F32)).astype(BF16)


def left_product(table, value):
    high, low = split(value)
    return dot(table, jnp.concatenate([high, low, high], axis=0))


def right_product(value, high_table, low_table):
    high, low = split(value)
    rows = value.shape[0]
    both = dot(jnp.concatenate([high, low], axis=0), high_table)
    return both[:rows] + both[rows:] + dot(high, low_table)


MESH = pl.DeviceIdType.MESH
STAGES = tuple(TABLES)


def chip_of(pair):
    place = (pair + 6) % 8
    row = place // 4
    return place + row * (7 - 2 * place), row


def computer_of(pair, core, member):
    x, row = chip_of(pair)
    return row * 8 + member % 8, x * 4 + member // 8 * 2 + core


def role_of(stick, band):
    row, x = stick // 8, band // 4
    place = x + row * (7 - 2 * x)
    return (place + 2) % 8, band % 2, band % 4 // 2 * 8 + stick % 8


def y_stage(field, high, low):
    return right_product(field, high, low)


def z_stage(field, table):
    starts = range(0, field.shape[0], ROWS)
    rows = [
        jnp.concatenate([field[a + G * z : a + G * (z + 1), 128 * y : 128 * (y + 1)] for z in range(3)], axis=1)
        for a in starts
        for y in range(6)
    ]
    high, low = split(jnp.concatenate(rows, axis=0))
    out = dot(jnp.concatenate([high, low, high], axis=1), table)
    return jnp.concatenate(
        [
            jnp.concatenate([out[2 * a + G * y : 2 * a + G * (y + 1), 128 * z : 128 * (z + 1)] for y in range(6)], axis=1)
            for a in starts
            for z in range(3)
        ],
        axis=0,
    )


def x_stage(field, table):
    return jnp.concatenate([left_product(table, field[G * z : G * (z + 1)]) for z in range(field.shape[0] // G)], axis=0)


def reflected(tiles):
    lane = lax.broadcasted_iota(jnp.int32, (G, 128), 1) // 16
    out = []
    for y in range(6):
        source = tiles[5 - y]
        turned = jnp.where(
            lane == 4,
            source,
            jnp.where(
                lane % 4 == 1,
                pltpu.roll(source, 32, 1),
                jnp.where(lane % 4 == 2, pltpu.roll(source, 64, 1), pltpu.roll(source, 96, 1)),
            ),
        )
        out.append(jnp.where(lane == 0, tiles[(6 - y) % 6], turned))
    return out


def slot_places(columns):
    kx = (columns * 43691) >> 21
    ky = columns - kx * G
    row = (ky >> 3) * G + kx
    return jnp.where(columns >= 0, row, -1), ky & 7


def one_hot(row):
    places = lax.broadcasted_iota(jnp.int32, (6 * G, row.shape[1]), 0)
    return jnp.where(places == row, 1.0, 0.0).astype(BF16)


def exchange_kernel(sticks, labels, *refs):
    count = len(STAGES)
    stored, out, held = refs[:count], refs[count], refs[count + 1 : 2 * count + 1]
    t = dict(zip(STAGES, held))
    (given, sent, blocks, columns, grid, fields, work, total, turned, found, back, ready, table_sem, in_send, in_recv,
     label_send, label_recv, field_send, field_recv, out_send, out_recv, out_store) = refs[2 * count + 1 :]
    stick, band = lax.axis_index("stick"), lax.axis_index("band")
    pair, core, member = role_of(stick, band)
    group = 2 * pair + core

    home = group == band
    own_row, own_column = computer_of(band // 2, band % 2, 0)

    def own_computer(i):
        return own_row + i % 8, own_column + i // 8 * 2

    upper, lower = (pair + 1) % 8, (pair + 7) % 8
    to_upper, to_lower = computer_of(upper, 0, member), computer_of(lower, 1, member)
    partner = computer_of(pair, 1 - core, member)
    beyond = core * upper + (1 - core) * lower
    from_first, from_second = computer_of(beyond, 0, member), computer_of(beyond, 1, member)

    barrier = pltpu.get_barrier_semaphore()

    def signal(device):
        pl.semaphore_signal(barrier, 1, device_id=device, device_id_type=MESH)

    def greet(i, carry):
        @pl.when(jnp.logical_not(jnp.logical_and(home, i == stick)))
        def _():
            signal((i, group))

        @pl.when(jnp.logical_not(jnp.logical_and(home, i == member)))
        def _():
            signal(own_computer(i))

        return carry

    lax.fori_loop(0, OWNERS, greet, 0)
    for device in (from_first, from_second, partner):
        signal(device)

    own_load = pltpu.make_async_copy(sticks, given, table_sem.at[count])
    own_load.start()
    loads = [pltpu.make_async_copy(a, b, table_sem.at[i]) for i, (a, b) in enumerate(zip(stored, held))]
    first_load = STAGES.index("z_in")
    loads[first_load].start()
    for i, load in enumerate(loads):
        if i != first_load:
            load.start()
    loads[first_load].wait()
    own_load.wait()

    pl.semaphore_wait(barrier, 2 * OWNERS + 3 - 2 * jnp.where(home, 1, 0))

    def either(same, device, source, target, out_sem, in_sem):
        here = jnp.logical_and(home, same)

        @pl.when(here)
        def _():
            pltpu.make_async_copy(source, target, in_sem).start()

        @pl.when(jnp.logical_not(here))
        def _():
            pltpu.make_async_remote_copy(
                source, target, out_sem, in_sem, device_id=device, device_id_type=MESH
            ).start()

    def label_copy(i):
        batch = (i + OWNERS - stick) % OWNERS // 4
        either(i == member, own_computer(i), labels, columns.at[stick], label_send.at[0], label_recv.at[batch])

    def plane_copy(z, i):
        batch = (i + OWNERS - stick) % OWNERS // 4
        source, target = sent.at[i, pl.ds(pl.multiple_of(32 * z, 32), 32)], blocks.at[z, stick]
        either(i == member, own_computer(i), source, target, in_send.at[0], in_recv.at[z, batch])

    def to_planes(step, carry):
        bands = [(stick + 2 * step + i) % OWNERS for i in range(2)]
        pair = jnp.concatenate([given[i] for i in bands], axis=1)
        pair = left_product(t["z_in"][...], pair)
        for i, band_index in enumerate(bands):
            sent[band_index] = pair[:, CAP * i : CAP * (i + 1)]
            label_copy(band_index)
            plane_copy(0, band_index)
        return carry

    def send_planes(index, carry):
        plane_copy(index // OWNERS, (stick + index) % OWNERS)
        return carry

    lax.fori_loop(0, OWNERS // 2, to_planes, 0)
    lax.fori_loop(OWNERS, 3 * OWNERS, send_planes, 0)

    spans = lax.broadcasted_iota(jnp.int32, (128, CAP), 0) >> 4

    def arrive(ref, sem):
        pltpu.make_async_copy(ref, ref, sem).wait()

    def field_copy(source, slot, z, device):
        return pltpu.make_async_remote_copy(
            fields.at[source, z],
            fields.at[slot, z],
            field_send.at[0],
            field_recv.at[slot - 1, z],
            device_id=device,
            device_id_type=MESH,
        )

    def outward(z):
        return [
            field_copy(0, 2 + core, z, to_upper),
            field_copy(0, 2 + core, z, to_lower),
            field_copy(0, 1, z, partner),
        ]

    def onward(z):
        return field_copy(3 - core, 4, z, partner)

    def pass_on(z):
        arrive(fields.at[3 - core, z], field_recv.at[2 - core, z])
        onward(z).start()

    def plane(z, carry):
        grid[...] = jnp.zeros_like(grid)

        def place(step, carry):
            owners = [(member + OWNERS - 4 * step - i) % OWNERS for i in range(4)]

            @pl.when(z == 0)
            def _():
                arrive(columns.at[pl.ds(0, 4)], label_recv.at[step])

            hots, spreads = [], []
            arrive(blocks.at[z, pl.ds(0, 4)], in_recv.at[z, step])
            for owner in owners:
                row, span = slot_places(columns[owner])
                keep = jnp.where(spans == span, 1.0, 0.0).astype(BF16)
                for part in split(blocks[z, owner]):
                    parts = [jnp.concatenate([part[16 * i : 16 * i + 16]] * 8, axis=0) * keep for i in range(2)]
                    spreads.append(jnp.concatenate(parts, axis=0))
                hots += [one_hot(row)] * 2
            grid[...] += lax.dot_general(
                jnp.concatenate(hots, axis=1),
                jnp.concatenate(spreads, axis=1),
                (((1,), (1,)), ((), ())),
                preferred_element_type=F32,
            )
            return carry

        lax.fori_loop(0, OWNERS // 4, place, 0)

        @pl.when(z == 0)
        def _():
            for i, load in enumerate(loads):
                if i != first_load:
                    load.wait()

        @pl.when(z == 2)
        def _():
            pass_on(0)

        real = [grid[G * y : G * (y + 1), :128] for y in range(6)]
        imag = [grid[G * y : G * (y + 1), 128:] for y in range(6)]
        first = jnp.concatenate([a - b for a, b in zip(reflected(real), imag)], axis=1)
        second = jnp.concatenate([a + b for a, b in zip(real, reflected(imag))], axis=1)
        both = y_stage(jnp.concatenate([first, second], axis=0), t["y_high"][...], t["y_low"][...])
        fields[0, z] = left_product(t["x_in"][...], both)
        for copy in outward(z):
            copy.start()

        return carry

    lax.fori_loop(0, 3, plane, 0)
    pass_on(1)

    own = fields[0].reshape(ROWS, WIDE)
    value = x_stage(own * own, t["x"][...])
    value = y_stage(value, t["y_high"][...], t["y_low"][...])
    value = z_stage(value, t["z"][...]) * t["kernel"][...]
    value = y_stage(z_stage(value, t["z"][...]), t["y_high"][...], t["y_low"][...])
    total[...] = (x_stage(value, t["x"][...]) * own).reshape(3, G, WIDE)

    def forward(z, carry):
        @pl.when(z == 1)
        def _():
            pass_on(2)

        arrive(fields.at[1, z], field_recv.at[0, z])
        arrive(fields.at[2 + core, z], field_recv.at[1 + core, z])
        arrive(fields.at[4, z], field_recv.at[3, z])
        value = jnp.concatenate([fields[0, z] * fields[slot, z] for slot in range(1, 5)], axis=0)
        value = y_stage(x_stage(value, t["x"][...]), t["y_high"][...], t["y_low"][...])
        for i in range(4):
            work[i, z] = value[G * i : G * (i + 1)]
        return carry

    lax.fori_loop(0, 3, forward, 0)
    value = z_stage(work[...].reshape(4 * ROWS, WIDE), t["z"][...])
    value = value * jnp.concatenate([t["kernel"][...]] * 4, axis=0)
    work[...] = z_stage(value, t["z"][...]).reshape(4, 3, G, WIDE)

    def result_copy(z, owner):
        batch = (member + OWNERS - owner) % OWNERS // 2
        source, target = found.at[z, owner], back.at[member, z]
        either(owner == stick, (owner, group), source, target, out_send.at[0], out_recv.at[batch])

    def backward(z, carry):
        value = jnp.concatenate([work[i, z] for i in range(4)], axis=0)
        value = x_stage(y_stage(value, t["y_high"][...], t["y_low"][...]), t["x"][...])
        field = total[z]
        for i in range(4):
            field = field + value[G * i : G * (i + 1)] * fields[i + 1, z]
        both = y_stage(left_product(t["x_out"][...], field), t["y_high"][...], t["y_low"][...])
        plus, minus = [[both[a : a + G, 128 * y : 128 * (y + 1)] for y in range(6)] for a in (0, G)]
        real = [a + b for a, b in zip(minus, reflected(plus))]
        imag = [a - b for a, b in zip(reflected(minus), plus)]
        for i, part in enumerate((real, imag)):
            high, low = split(jnp.concatenate(part, axis=0).T)
            turned[128 * i : 128 * (i + 1), : 6 * G] = high
            turned[128 * i : 128 * (i + 1), 6 * G :] = low

        def pick(step, carry):
            owners = [(member + OWNERS - 2 * step - i) % OWNERS for i in range(2)]
            row, span = slot_places(jnp.concatenate([columns[owner] for owner in owners], axis=1))
            hot = one_hot(row)
            picked = dot(turned[...], jnp.concatenate([hot, hot], axis=0))
            rows = []
            for i in range(2):
                value = jnp.zeros((16, 2 * CAP), F32)
                for g in range(8):
                    start = 128 * i + 16 * g
                    value = value + jnp.where(span == g, picked[start : start + 16], 0.0)
                rows.append(value)
            result = jnp.concatenate(rows, axis=0)
            for i, owner in enumerate(owners):
                found[z, owner] = result[:, CAP * i : CAP * (i + 1)]
                result_copy(z, owner)
            return carry

        lax.fori_loop(0, OWNERS // 2, pick, 0)
        return carry

    lax.fori_loop(0, 3, backward, 0)

    def from_planes(step, carry):
        bands = [(stick + 2 * step + i) % OWNERS for i in range(2)]
        arrive(back.at[pl.ds(0, 2)], out_recv.at[step])
        pair = jnp.concatenate([back[band_index].reshape(2 * G, CAP) for band_index in bands], axis=1)
        pair = left_product(t["z_out"][...], pair)
        for i, band_index in enumerate(bands):
            ready[band_index] = pair[:, CAP * i : CAP * (i + 1)]
            pltpu.make_async_copy(ready.at[band_index], out.at[band_index], out_store.at[0]).start()
        return carry

    lax.fori_loop(0, OWNERS // 2, from_planes, 0)
    arrive(fields.at[pl.ds(0, 4)], field_send.at[0])

    @pl.when(home)
    def _():
        arrive(sent.at[pl.ds(0, OWNERS - 1)], in_send.at[0])
        arrive(columns.at[pl.ds(0, OWNERS - 1)], label_send.at[0])
        arrive(found.at[:, pl.ds(0, OWNERS - 1)], out_send.at[0])

    @pl.when(jnp.logical_not(home))
    def _():
        arrive(sent, in_send.at[0])
        arrive(columns, label_send.at[0])
        arrive(found, out_send.at[0])

    pltpu.make_async_copy(ready, out, out_store.at[0]).wait()


def on_device(sticks, stick_columns):
    tables = [jnp.asarray(TABLES[name]) for name in STAGES]
    anywhere, hbm = pl.BlockSpec(memory_space=pl.ANY), pl.BlockSpec(memory_space=pltpu.HBM)
    dma = pltpu.SemaphoreType.DMA
    result = pl.pallas_call(
        exchange_kernel,
        out_shape=jax.ShapeDtypeStruct((OWNERS, 2 * G, CAP), F32),
        in_specs=[hbm] * (2 + len(tables)),
        out_specs=anywhere,
        scratch_shapes=[pltpu.VMEM(t.shape, t.dtype) for t in tables]
        + [
            pltpu.VMEM((OWNERS, 2 * G, CAP), F32),
            pltpu.VMEM((OWNERS, 2 * G, CAP), F32),
            pltpu.VMEM((3, OWNERS, 32, CAP), F32),
            pltpu.VMEM((OWNERS, 1, CAP), jnp.int32),
            pltpu.VMEM((6 * G, 256), F32),
            pltpu.VMEM((5, 3, G, WIDE), F32),
            pltpu.VMEM((4, 3, G, WIDE), F32),
            pltpu.VMEM((3, G, WIDE), F32),
            pltpu.VMEM((256, 12 * G), BF16),
            pltpu.VMEM((3, OWNERS, 32, CAP), F32),
            pltpu.VMEM((OWNERS, 3, 32, CAP), F32),
            pltpu.VMEM((OWNERS, 2 * G, CAP), F32),
            dma((len(tables) + 1,)),
            dma((1,)),
            dma((3, 4)),
            dma((1,)),
            dma((4,)),
            dma((1,)),
            dma((4, 3)),
            dma((1,)),
            dma((OWNERS // 2,)),
            dma((1,)),
        ],
        compiler_params=pltpu.CompilerParams(collective_id=0, has_side_effects=True, vmem_limit_bytes=48 << 20),
    )(*[pltpu.with_memory_space_constraint(a, pltpu.HBM) for a in (sticks, stick_columns.reshape(1, CAP), *tables)])
    return result * np.float32(G**-1.5)


def solution(mesh):
    return jax.shard_map(
        on_device,
        mesh=mesh,
        in_specs=(P("band", None, "stick"), P("stick")),
        out_specs=P("band", None, "stick"),
        check_vma=False,
    )
```

```python
import functools
import math

import jax
import jax.numpy as jnp
import ml_dtypes
import numpy as np
from jax import lax
from jax.experimental import pallas as pl
from jax.experimental.pallas import tpu as pltpu
from jax.sharding import PartitionSpec as P

G = 48
ROWS, WIDE = 3 * G, 16 * G
OWNERS = 16
CAP = 128
BOX_LENGTH = 18.0
F32, BF16 = jnp.float32, jnp.bfloat16


def two_parts(table):
    high = table.astype(ml_dtypes.bfloat16)
    low = (table - high.astype(np.float64)).astype(ml_dtypes.bfloat16)
    return high, low


def stacked(table):
    high, low = two_parts(table)
    return np.concatenate([high, high, low], axis=1)


def make_tables():
    index = np.arange(G)
    angle = 2.0 * np.pi / G * (np.outer(index, index) % G)
    cos, sin = np.cos(angle), np.sin(angle)
    plus = (cos + sin) / np.sqrt(G)
    minus = (cos - sin) / np.sqrt(G)
    on_y = np.kron(plus, np.eye(16))
    on_z = np.einsum("aibj,kl->akiblj", plus.reshape(3, 16, 3, 16), np.eye(8)).reshape(384, 384)
    folded = np.minimum(index, G - index).astype(np.float64) ** 2
    total = folded[:, None, None] + folded[None, :, None] + folded[None, None, :]
    kernel = np.where(total > 0, 4.0 * np.pi / ((2.0 * np.pi / BOX_LENGTH) ** 2 * np.maximum(total, 1.0)), 0.0)
    kernel = kernel.reshape(G, 6, 8, 3, 16).transpose(3, 0, 1, 2, 4).reshape(ROWS, WIDE)
    z_in = np.block([[cos, -sin], [sin, cos]]).reshape(2, 3, 16, 2 * G).transpose(1, 0, 2, 3).reshape(2 * G, 2 * G)
    z_out = np.block([[cos, sin], [-sin, cos]]).reshape(2 * G, 2, 3, 16).transpose(0, 2, 1, 3).reshape(2 * G, 2 * G)
    return dict(
        x=stacked(plus),
        x_in=stacked(np.concatenate([plus, minus], axis=1) * (0.5 * G)),
        x_out=stacked(np.concatenate([plus, minus], axis=0) * (0.5 * G)),
        y_high=two_parts(on_y)[0],
        y_low=two_parts(on_y)[1],
        z=stacked(on_z.T).T.copy(),
        kernel=kernel.astype(np.float32),
        z_in=stacked(z_in),
        z_out=stacked(z_out),
    )


TABLES = make_tables()


def dot(left, right):
    return jnp.dot(left, right, preferred_element_type=F32)


def split(value):
    high = value.astype(BF16)
    return high, (value - high.astype(F32)).astype(BF16)


def left_product(table, value):
    high, low = split(value)
    return dot(table, jnp.concatenate([high, low, high], axis=0))


def right_product(value, high_table, low_table):
    high, low = split(value)
    rows = value.shape[0]
    both = dot(jnp.concatenate([high, low], axis=0), high_table)
    return both[:rows] + both[rows:] + dot(high, low_table)


MESH = pl.DeviceIdType.MESH
STAGES = tuple(TABLES)


def chip_of(pair):
    place = (pair + 6) % 8
    row = place // 4
    return place + row * (7 - 2 * place), row


def computer_of(pair, core, member):
    x, row = chip_of(pair)
    return row * 8 + member % 8, x * 4 + member // 8 * 2 + core


def role_of(stick, band):
    row, x = stick // 8, band // 4
    place = x + row * (7 - 2 * x)
    return (place + 2) % 8, band % 2, band % 4 // 2 * 8 + stick % 8


def y_stage(field, high, low):
    return right_product(field, high, low)


def z_stage(field, table):
    starts = range(0, field.shape[0], ROWS)
    rows = [
        jnp.concatenate([field[a + G * z : a + G * (z + 1), 128 * y : 128 * (y + 1)] for z in range(3)], axis=1)
        for a in starts
        for y in range(6)
    ]
    high, low = split(jnp.concatenate(rows, axis=0))
    out = dot(jnp.concatenate([high, low, high], axis=1), table)
    return jnp.concatenate(
        [
            jnp.concatenate([out[2 * a + G * y : 2 * a + G * (y + 1), 128 * z : 128 * (z + 1)] for y in range(6)], axis=1)
            for a in starts
            for z in range(3)
        ],
        axis=0,
    )


def x_stage(field, table):
    return jnp.concatenate([left_product(table, field[G * z : G * (z + 1)]) for z in range(field.shape[0] // G)], axis=0)


def reflected(tiles):
    lane = lax.broadcasted_iota(jnp.int32, (G, 128), 1) // 16
    out = []
    for y in range(6):
        source = tiles[5 - y]
        turned = jnp.where(
            lane == 4,
            source,
            jnp.where(
                lane % 4 == 1,
                pltpu.roll(source, 32, 1),
                jnp.where(lane % 4 == 2, pltpu.roll(source, 64, 1), pltpu.roll(source, 96, 1)),
            ),
        )
        out.append(jnp.where(lane == 0, tiles[(6 - y) % 6], turned))
    return out


def slot_places(columns):
    kx = (columns * 43691) >> 21
    ky = columns - kx * G
    row = (ky >> 3) * G + kx
    return jnp.where(columns >= 0, row, -1), ky & 7


def one_hot(row):
    places = lax.broadcasted_iota(jnp.int32, (6 * G, row.shape[1]), 0)
    return jnp.where(places == row, 1.0, 0.0).astype(BF16)


def exchange_kernel(sticks, labels, *refs):
    count = len(STAGES)
    stored, out, held = refs[:count], refs[count], refs[count + 1 : 2 * count + 1]
    t = dict(zip(STAGES, held))
    (given, sent, blocks, columns, grid, fields, work, total, turned, found, back, ready, table_sem, in_send, in_recv,
     label_send, label_recv, field_send, field_recv, out_send, out_recv, out_store) = refs[2 * count + 1 :]
    stick, band = lax.axis_index("stick"), lax.axis_index("band")
    pair, core, member = role_of(stick, band)
    group = 2 * pair + core

    home = group == band
    own_row, own_column = computer_of(band // 2, band % 2, 0)

    def own_computer(i):
        return own_row + i % 8, own_column + i // 8 * 2

    upper, lower = (pair + 1) % 8, (pair + 7) % 8
    to_upper, to_lower = computer_of(upper, 0, member), computer_of(lower, 1, member)
    partner = computer_of(pair, 1 - core, member)
    beyond = core * upper + (1 - core) * lower
    from_first, from_second = computer_of(beyond, 0, member), computer_of(beyond, 1, member)
    to_same, from_same = computer_of(beyond, core, member), computer_of((2 * pair + 8 - beyond) % 8, core, member)

    barrier = pltpu.get_barrier_semaphore()

    def signal(device):
        pl.semaphore_signal(barrier, 1, device_id=device, device_id_type=MESH)

    def greet(i, carry):
        @pl.when(jnp.logical_not(jnp.logical_and(home, i == stick)))
        def _():
            signal((i, group))

        @pl.when(jnp.logical_not(jnp.logical_and(home, i == member)))
        def _():
            signal(own_computer(i))

        return carry

    lax.fori_loop(0, OWNERS, greet, 0)
    for device in (from_first, from_second, from_same, partner):
        signal(device)

    own_load = pltpu.make_async_copy(sticks, given, table_sem.at[count])
    own_load.start()
    loads = [pltpu.make_async_copy(a, b, table_sem.at[i]) for i, (a, b) in enumerate(zip(stored, held))]
    first_load = STAGES.index("z_in")
    loads[first_load].start()
    for i, load in enumerate(loads):
        if i != first_load:
            load.start()
    loads[first_load].wait()
    own_load.wait()

    pl.semaphore_wait(barrier, 2 * OWNERS + 4 - 2 * jnp.where(home, 1, 0))

    def either(same, device, source, target, out_sem, in_sem):
        here = jnp.logical_and(home, same)

        @pl.when(here)
        def _():
            pltpu.make_async_copy(source, target, in_sem).start()

        @pl.when(jnp.logical_not(here))
        def _():
            pltpu.make_async_remote_copy(
                source, target, out_sem, in_sem, device_id=device, device_id_type=MESH
            ).start()

    def label_copy(i):
        batch = (i + OWNERS - stick) % OWNERS // 4
        either(i == member, own_computer(i), labels, columns.at[stick], label_send.at[0], label_recv.at[batch])

    def plane_copy(z, i):
        batch = (i + OWNERS - stick) % OWNERS // 4
        source, target = sent.at[i, pl.ds(pl.multiple_of(32 * z, 32), 32)], blocks.at[z, stick]
        either(i == member, own_computer(i), source, target, in_send.at[0], in_recv.at[z, batch])

    def to_planes(step, carry):
        bands = [(stick + 2 * step + i) % OWNERS for i in range(2)]
        pair = jnp.concatenate([given[i] for i in bands], axis=1)
        pair = left_product(t["z_in"][...], pair)
        for i, band_index in enumerate(bands):
            sent[band_index] = pair[:, CAP * i : CAP * (i + 1)]
            label_copy(band_index)
            plane_copy(0, band_index)
        return carry

    def send_planes(index, carry):
        plane_copy(index // OWNERS, (stick + index) % OWNERS)
        return carry

    lax.fori_loop(0, OWNERS // 2, to_planes, 0)
    lax.fori_loop(OWNERS, 3 * OWNERS, send_planes, 0)

    spans = lax.broadcasted_iota(jnp.int32, (128, CAP), 0) >> 4

    def arrive(ref, sem):
        pltpu.make_async_copy(ref, ref, sem).wait()

    def field_copy(source, slot, z, device):
        return pltpu.make_async_remote_copy(
            fields.at[source, z],
            fields.at[slot, z],
            field_send.at[0],
            field_recv.at[slot - 1, z],
            device_id=device,
            device_id_type=MESH,
        )

    def outward(z):
        return [
            field_copy(0, 2 + core, z, to_upper),
            field_copy(0, 2 + core, z, to_lower),
            field_copy(0, 1, z, partner),
        ]

    def onward(z):
        return field_copy(3 - core, 4, z, partner)

    def pass_on(z):
        arrive(fields.at[3 - core, z], field_recv.at[2 - core, z])
        onward(z).start()

    def plane(z, carry):
        grid[...] = jnp.zeros_like(grid)

        def place(step, carry):
            owners = [(member + OWNERS - 4 * step - i) % OWNERS for i in range(4)]

            @pl.when(z == 0)
            def _():
                arrive(columns.at[pl.ds(0, 4)], label_recv.at[step])

            hots, spreads = [], []
            arrive(blocks.at[z, pl.ds(0, 4)], in_recv.at[z, step])
            for owner in owners:
                row, span = slot_places(columns[owner])
                keep = jnp.where(spans == span, 1.0, 0.0).astype(BF16)
                for part in split(blocks[z, owner]):
                    parts = [jnp.concatenate([part[16 * i : 16 * i + 16]] * 8, axis=0) * keep for i in range(2)]
                    spreads.append(jnp.concatenate(parts, axis=0))
                hots += [one_hot(row)] * 2
            grid[...] += lax.dot_general(
                jnp.concatenate(hots, axis=1),
                jnp.concatenate(spreads, axis=1),
                (((1,), (1,)), ((), ())),
                preferred_element_type=F32,
            )
            return carry

        lax.fori_loop(0, OWNERS // 4, place, 0)

        @pl.when(z == 0)
        def _():
            for i, load in enumerate(loads):
                if i != first_load:
                    load.wait()

        @pl.when(z == 2)
        def _():
            pass_on(0)

        real = [grid[G * y : G * (y + 1), :128] for y in range(6)]
        imag = [grid[G * y : G * (y + 1), 128:] for y in range(6)]
        first = jnp.concatenate([a - b for a, b in zip(reflected(real), imag)], axis=1)
        second = jnp.concatenate([a + b for a, b in zip(real, reflected(imag))], axis=1)
        both = y_stage(jnp.concatenate([first, second], axis=0), t["y_high"][...], t["y_low"][...])
        fields[0, z] = left_product(t["x_in"][...], both)
        for copy in outward(z):
            copy.start()

        @pl.when(z == 2)
        def _():
            field_copy(0, 4, z, to_same).start()

        return carry

    lax.fori_loop(0, 3, plane, 0)
    own = fields[0].reshape(ROWS, WIDE)
    value = x_stage(own * own, t["x"][...])
    value = y_stage(value, t["y_high"][...], t["y_low"][...])
    value = z_stage(value, t["z"][...]) * t["kernel"][...]
    work[0] = value.reshape(3, G, WIDE)
    pass_on(1)
    value = work[0].reshape(ROWS, WIDE)
    value = y_stage(z_stage(value, t["z"][...]), t["y_high"][...], t["y_low"][...])
    total[...] = (x_stage(value, t["x"][...]) * own).reshape(3, G, WIDE)

    def forward(z, carry):
        @pl.when(z == 2)
        def _():
            arrive(fields.at[3 - core, z], field_recv.at[2 - core, z])

        arrive(fields.at[1, z], field_recv.at[0, z])
        arrive(fields.at[2 + core, z], field_recv.at[1 + core, z])
        arrive(fields.at[4, z], field_recv.at[3, z])
        value = jnp.concatenate([fields[0, z] * fields[slot, z] for slot in range(1, 5)], axis=0)
        value = y_stage(x_stage(value, t["x"][...]), t["y_high"][...], t["y_low"][...])
        for i in range(4):
            work[i, z] = value[G * i : G * (i + 1)]
        return carry

    lax.fori_loop(0, 3, forward, 0)
    value = z_stage(work[...].reshape(4 * ROWS, WIDE), t["z"][...])
    value = value * jnp.concatenate([t["kernel"][...]] * 4, axis=0)
    work[...] = z_stage(value, t["z"][...]).reshape(4, 3, G, WIDE)

    def result_copy(z, owner):
        batch = (member + OWNERS - owner) % OWNERS // 2
        source, target = found.at[z, owner], back.at[member, z]
        either(owner == stick, (owner, group), source, target, out_send.at[0], out_recv.at[batch])

    def backward(z, carry):
        value = jnp.concatenate([work[i, z] for i in range(4)], axis=0)
        value = x_stage(y_stage(value, t["y_high"][...], t["y_low"][...]), t["x"][...])
        field = total[z]
        for i in range(4):
            field = field + value[G * i : G * (i + 1)] * fields[i + 1, z]
        both = y_stage(left_product(t["x_out"][...], field), t["y_high"][...], t["y_low"][...])
        plus, minus = [[both[a : a + G, 128 * y : 128 * (y + 1)] for y in range(6)] for a in (0, G)]
        real = [a + b for a, b in zip(minus, reflected(plus))]
        imag = [a - b for a, b in zip(reflected(minus), plus)]
        for i, part in enumerate((real, imag)):
            high, low = split(jnp.concatenate(part, axis=0).T)
            turned[128 * i : 128 * (i + 1), : 6 * G] = high
            turned[128 * i : 128 * (i + 1), 6 * G :] = low

        def pick(step, carry):
            owners = [(member + OWNERS - 2 * step - i) % OWNERS for i in range(2)]
            row, span = slot_places(jnp.concatenate([columns[owner] for owner in owners], axis=1))
            hot = one_hot(row)
            picked = dot(turned[...], jnp.concatenate([hot, hot], axis=0))
            rows = []
            for i in range(2):
                value = jnp.zeros((16, 2 * CAP), F32)
                for g in range(8):
                    start = 128 * i + 16 * g
                    value = value + jnp.where(span == g, picked[start : start + 16], 0.0)
                rows.append(value)
            result = jnp.concatenate(rows, axis=0)
            for i, owner in enumerate(owners):
                found[z, owner] = result[:, CAP * i : CAP * (i + 1)]
                result_copy(z, owner)
            return carry

        lax.fori_loop(0, OWNERS // 2, pick, 0)
        return carry

    lax.fori_loop(0, 3, backward, 0)

    def from_planes(step, carry):
        bands = [(stick + 2 * step + i) % OWNERS for i in range(2)]
        arrive(back.at[pl.ds(0, 2)], out_recv.at[step])
        pair = jnp.concatenate([back[band_index].reshape(2 * G, CAP) for band_index in bands], axis=1)
        pair = left_product(t["z_out"][...], pair)
        for i, band_index in enumerate(bands):
            ready[band_index] = pair[:, CAP * i : CAP * (i + 1)]
            pltpu.make_async_copy(ready.at[band_index], out.at[band_index], out_store.at[0]).start()
        return carry

    lax.fori_loop(0, OWNERS // 2, from_planes, 0)
    arrive(fields.at[pl.ds(0, 4)], field_send.at[0])

    @pl.when(home)
    def _():
        arrive(sent.at[pl.ds(0, OWNERS - 1)], in_send.at[0])
        arrive(columns.at[pl.ds(0, OWNERS - 1)], label_send.at[0])
        arrive(found.at[:, pl.ds(0, OWNERS - 1)], out_send.at[0])

    @pl.when(jnp.logical_not(home))
    def _():
        arrive(sent, in_send.at[0])
        arrive(columns, label_send.at[0])
        arrive(found, out_send.at[0])

    pltpu.make_async_copy(ready, out, out_store.at[0]).wait()


def on_device(sticks, stick_columns):
    tables = [jnp.asarray(TABLES[name]) for name in STAGES]
    anywhere, hbm = pl.BlockSpec(memory_space=pl.ANY), pl.BlockSpec(memory_space=pltpu.HBM)
    dma = pltpu.SemaphoreType.DMA
    result = pl.pallas_call(
        exchange_kernel,
        out_shape=jax.ShapeDtypeStruct((OWNERS, 2 * G, CAP), F32),
        in_specs=[hbm] * (2 + len(tables)),
        out_specs=anywhere,
        scratch_shapes=[pltpu.VMEM(t.shape, t.dtype) for t in tables]
        + [
            pltpu.VMEM((OWNERS, 2 * G, CAP), F32),
            pltpu.VMEM((OWNERS, 2 * G, CAP), F32),
            pltpu.VMEM((3, OWNERS, 32, CAP), F32),
            pltpu.VMEM((OWNERS, 1, CAP), jnp.int32),
            pltpu.VMEM((6 * G, 256), F32),
            pltpu.VMEM((5, 3, G, WIDE), F32),
            pltpu.VMEM((4, 3, G, WIDE), F32),
            pltpu.VMEM((3, G, WIDE), F32),
            pltpu.VMEM((256, 12 * G), BF16),
            pltpu.VMEM((3, OWNERS, 32, CAP), F32),
            pltpu.VMEM((OWNERS, 3, 32, CAP), F32),
            pltpu.VMEM((OWNERS, 2 * G, CAP), F32),
            dma((len(tables) + 1,)),
            dma((1,)),
            dma((3, 4)),
            dma((1,)),
            dma((4,)),
            dma((1,)),
            dma((4, 3)),
            dma((1,)),
            dma((OWNERS // 2,)),
            dma((1,)),
        ],
        compiler_params=pltpu.CompilerParams(collective_id=0, has_side_effects=True, vmem_limit_bytes=48 << 20),
    )(*[pltpu.with_memory_space_constraint(a, pltpu.HBM) for a in (sticks, stick_columns.reshape(1, CAP), *tables)])
    return result * np.float32(G**-1.5)


def solution(mesh):
    return jax.shard_map(
        on_device,
        mesh=mesh,
        in_specs=(P("band", None, "stick"), P("stick")),
        out_specs=P("band", None, "stick"),
        check_vma=False,
    )
```

```python
import functools
import math

import jax
import jax.numpy as jnp
import ml_dtypes
import numpy as np
from jax import lax
from jax.experimental import pallas as pl
from jax.experimental.pallas import tpu as pltpu
from jax.sharding import PartitionSpec as P

G = 48
ROWS, WIDE = 3 * G, 16 * G
OWNERS = 16
CAP = 128
BOX_LENGTH = 18.0
F32, BF16 = jnp.float32, jnp.bfloat16


def two_parts(table):
    high = table.astype(ml_dtypes.bfloat16)
    low = (table - high.astype(np.float64)).astype(ml_dtypes.bfloat16)
    return high, low


def stacked(table):
    high, low = two_parts(table)
    return np.concatenate([high, high, low], axis=1)


def make_tables():
    index = np.arange(G)
    angle = 2.0 * np.pi / G * (np.outer(index, index) % G)
    cos, sin = np.cos(angle), np.sin(angle)
    plus = (cos + sin) / np.sqrt(G)
    minus = (cos - sin) / np.sqrt(G)
    on_y = np.kron(plus, np.eye(16))
    on_z = np.einsum("aibj,kl->akiblj", plus.reshape(3, 16, 3, 16), np.eye(8)).reshape(384, 384)
    folded = np.minimum(index, G - index).astype(np.float64) ** 2
    total = folded[:, None, None] + folded[None, :, None] + folded[None, None, :]
    kernel = np.where(total > 0, 4.0 * np.pi / ((2.0 * np.pi / BOX_LENGTH) ** 2 * np.maximum(total, 1.0)), 0.0)
    kernel = kernel.reshape(G, 6, 8, 3, 16).transpose(3, 0, 1, 2, 4).reshape(ROWS, WIDE)
    z_in = np.block([[cos, -sin], [sin, cos]]).reshape(2, 3, 16, 2 * G).transpose(1, 0, 2, 3).reshape(2 * G, 2 * G)
    z_out = np.block([[cos, sin], [-sin, cos]]).reshape(2 * G, 2, 3, 16).transpose(0, 2, 1, 3).reshape(2 * G, 2 * G)
    return dict(
        x=stacked(plus),
        x_in=stacked(np.concatenate([plus, minus], axis=1) * (0.5 * G)),
        x_out=stacked(np.concatenate([plus, minus], axis=0) * (0.5 * G)),
        y_high=two_parts(on_y)[0],
        y_low=two_parts(on_y)[1],
        z=stacked(on_z.T).T.copy(),
        kernel=kernel.astype(np.float32),
        z_in=stacked(z_in),
        z_out=stacked(z_out),
    )


TABLES = make_tables()


def dot(left, right):
    return jnp.dot(left, right, preferred_element_type=F32)


def split(value):
    high = value.astype(BF16)
    return high, (value - high.astype(F32)).astype(BF16)


def left_product(table, value):
    high, low = split(value)
    return dot(table, jnp.concatenate([high, low, high], axis=0))


def right_product(value, high_table, low_table):
    high, low = split(value)
    rows = value.shape[0]
    both = dot(jnp.concatenate([high, low], axis=0), high_table)
    return both[:rows] + both[rows:] + dot(high, low_table)


MESH = pl.DeviceIdType.MESH
STAGES = tuple(TABLES)


def chip_of(pair):
    place = (pair + 6) % 8
    row = place // 4
    return place + row * (7 - 2 * place), row


def computer_of(pair, core, member):
    x, row = chip_of(pair)
    return row * 8 + member % 8, x * 4 + member // 8 * 2 + core


def role_of(stick, band):
    row, x = stick // 8, band // 4
    place = x + row * (7 - 2 * x)
    return (place + 2) % 8, band % 2, band % 4 // 2 * 8 + stick % 8


def y_stage(field, high, low):
    return right_product(field, high, low)


def z_stage(field, table):
    starts = range(0, field.shape[0], ROWS)
    rows = [
        jnp.concatenate([field[a + G * z : a + G * (z + 1), 128 * y : 128 * (y + 1)] for z in range(3)], axis=1)
        for a in starts
        for y in range(6)
    ]
    high, low = split(jnp.concatenate(rows, axis=0))
    out = dot(jnp.concatenate([high, low, high], axis=1), table)
    return jnp.concatenate(
        [
            jnp.concatenate([out[2 * a + G * y : 2 * a + G * (y + 1), 128 * z : 128 * (z + 1)] for y in range(6)], axis=1)
            for a in starts
            for z in range(3)
        ],
        axis=0,
    )


def x_stage(field, table):
    return jnp.concatenate([left_product(table, field[G * z : G * (z + 1)]) for z in range(field.shape[0] // G)], axis=0)


def reflected(tiles):
    lane = lax.broadcasted_iota(jnp.int32, (G, 128), 1) // 16
    out = []
    for y in range(6):
        source = tiles[5 - y]
        turned = jnp.where(
            lane == 4,
            source,
            jnp.where(
                lane % 4 == 1,
                pltpu.roll(source, 32, 1),
                jnp.where(lane % 4 == 2, pltpu.roll(source, 64, 1), pltpu.roll(source, 96, 1)),
            ),
        )
        out.append(jnp.where(lane == 0, tiles[(6 - y) % 6], turned))
    return out


def slot_places(columns):
    kx = (columns * 43691) >> 21
    ky = columns - kx * G
    row = (ky >> 3) * G + kx
    return jnp.where(columns >= 0, row, -1), ky & 7


def one_hot(row):
    places = lax.broadcasted_iota(jnp.int32, (6 * G, row.shape[1]), 0)
    return jnp.where(places == row, 1.0, 0.0).astype(BF16)


def exchange_kernel(sticks, labels, *refs):
    count = len(STAGES)
    stored, out, held = refs[:count], refs[count], refs[count + 1 : 2 * count + 1]
    t = dict(zip(STAGES, held))
    (given, sent, blocks, columns, grid, fields, work, total, turned, found, back, ready, table_sem, in_send, in_recv,
     label_send, label_recv, field_send, field_recv, out_send, out_recv, out_store) = refs[2 * count + 1 :]
    stick, band = lax.axis_index("stick"), lax.axis_index("band")
    pair, core, member = role_of(stick, band)
    group = 2 * pair + core

    home = group == band
    own_row, own_column = computer_of(band // 2, band % 2, 0)

    def own_computer(i):
        return own_row + i % 8, own_column + i // 8 * 2

    upper, lower = (pair + 1) % 8, (pair + 7) % 8
    to_upper, to_lower = computer_of(upper, 0, member), computer_of(lower, 1, member)
    partner = computer_of(pair, 1 - core, member)
    beyond = core * upper + (1 - core) * lower
    from_first, from_second = computer_of(beyond, 0, member), computer_of(beyond, 1, member)
    to_same, from_same = computer_of(beyond, core, member), computer_of((2 * pair + 8 - beyond) % 8, core, member)

    barrier = pltpu.get_barrier_semaphore()

    def signal(device):
        pl.semaphore_signal(barrier, 1, device_id=device, device_id_type=MESH)

    def greet(i, carry):
        @pl.when(jnp.logical_not(jnp.logical_and(home, i == stick)))
        def _():
            signal((i, group))

        @pl.when(jnp.logical_not(jnp.logical_and(home, i == member)))
        def _():
            signal(own_computer(i))

        return carry

    lax.fori_loop(0, OWNERS, greet, 0)
    for device in (from_first, from_second, from_same, partner):
        signal(device)

    own_load = pltpu.make_async_copy(sticks, given, table_sem.at[count])
    own_load.start()
    loads = [pltpu.make_async_copy(a, b, table_sem.at[i]) for i, (a, b) in enumerate(zip(stored, held))]
    first_load = STAGES.index("z_in")
    loads[first_load].start()
    for i, load in enumerate(loads):
        if i != first_load:
            load.start()
    loads[first_load].wait()
    own_load.wait()

    pl.semaphore_wait(barrier, 2 * OWNERS + 4 - 2 * jnp.where(home, 1, 0))

    def either(same, device, source, target, out_sem, in_sem):
        here = jnp.logical_and(home, same)

        @pl.when(here)
        def _():
            pltpu.make_async_copy(source, target, in_sem).start()

        @pl.when(jnp.logical_not(here))
        def _():
            pltpu.make_async_remote_copy(
                source, target, out_sem, in_sem, device_id=device, device_id_type=MESH
            ).start()

    def label_copy(i):
        batch = (i + OWNERS - stick) % OWNERS // 4
        either(i == member, own_computer(i), labels, columns.at[stick], label_send.at[0], label_recv.at[batch])

    def plane_copy(z, i):
        batch = (i + OWNERS - stick) % OWNERS // 4
        source, target = sent.at[i, pl.ds(pl.multiple_of(32 * z, 32), 32)], blocks.at[z, stick]
        either(i == member, own_computer(i), source, target, in_send.at[0], in_recv.at[z, batch])

    def to_planes(step, carry):
        bands = [(stick + 2 * step + i) % OWNERS for i in range(2)]
        pair = jnp.concatenate([given[i] for i in bands], axis=1)
        pair = left_product(t["z_in"][...], pair)
        for i, band_index in enumerate(bands):
            sent[band_index] = pair[:, CAP * i : CAP * (i + 1)]
            label_copy(band_index)
            plane_copy(0, band_index)
        return carry

    def send_planes(index, carry):
        plane_copy(index // OWNERS, (stick + index) % OWNERS)
        return carry

    lax.fori_loop(0, OWNERS // 2, to_planes, 0)
    lax.fori_loop(OWNERS, 3 * OWNERS, send_planes, 0)

    spans = lax.broadcasted_iota(jnp.int32, (128, CAP), 0) >> 4

    def arrive(ref, sem):
        pltpu.make_async_copy(ref, ref, sem).wait()

    def field_copy(source, slot, z, device):
        return pltpu.make_async_remote_copy(
            fields.at[source, z],
            fields.at[slot, z],
            field_send.at[0],
            field_recv.at[slot - 1, z],
            device_id=device,
            device_id_type=MESH,
        )

    def outward(z):
        return [
            field_copy(0, 2 + core, z, to_upper),
            field_copy(0, 2 + core, z, to_lower),
            field_copy(0, 1, z, partner),
        ]

    def onward(z):
        return field_copy(3 - core, 4, z, partner)

    def pass_on(z):
        arrive(fields.at[3 - core, z], field_recv.at[2 - core, z])
        onward(z).start()

    def plane(z, carry):
        grid[...] = jnp.zeros_like(grid)

        def place(step, carry):
            owners = [(member + OWNERS - 4 * step - i) % OWNERS for i in range(4)]

            @pl.when(z == 0)
            def _():
                arrive(columns.at[pl.ds(0, 4)], label_recv.at[step])

            hots, spreads = [], []
            arrive(blocks.at[z, pl.ds(0, 4)], in_recv.at[z, step])
            for owner in owners:
                row, span = slot_places(columns[owner])
                keep = jnp.where(spans == span, 1.0, 0.0).astype(BF16)
                for part in split(blocks[z, owner]):
                    parts = [jnp.concatenate([part[16 * i : 16 * i + 16]] * 8, axis=0) * keep for i in range(2)]
                    spreads.append(jnp.concatenate(parts, axis=0))
                hots += [one_hot(row)] * 2
            grid[...] += lax.dot_general(
                jnp.concatenate(hots, axis=1),
                jnp.concatenate(spreads, axis=1),
                (((1,), (1,)), ((), ())),
                preferred_element_type=F32,
            )
            return carry

        lax.fori_loop(0, OWNERS // 4, place, 0)

        @pl.when(z == 0)
        def _():
            for i, load in enumerate(loads):
                if i != first_load:
                    load.wait()

        real = [grid[G * y : G * (y + 1), :128] for y in range(6)]
        imag = [grid[G * y : G * (y + 1), 128:] for y in range(6)]
        first = jnp.concatenate([a - b for a, b in zip(reflected(real), imag)], axis=1)
        second = jnp.concatenate([a + b for a, b in zip(real, reflected(imag))], axis=1)
        both = y_stage(jnp.concatenate([first, second], axis=0), t["y_high"][...], t["y_low"][...])
        fields[0, z] = left_product(t["x_in"][...], both)
        for copy in outward(z):
            copy.start()

        @pl.when(z == 2)
        def _():
            field_copy(0, 4, z, to_same).start()

        return carry

    lax.fori_loop(0, 3, plane, 0)
    pass_on(0)
    own = fields[0].reshape(ROWS, WIDE)
    value = x_stage(own * own, t["x"][...])
    value = y_stage(value, t["y_high"][...], t["y_low"][...])
    value = z_stage(value, t["z"][...]) * t["kernel"][...]
    work[0] = value.reshape(3, G, WIDE)
    pass_on(1)
    value = work[0].reshape(ROWS, WIDE)
    value = y_stage(z_stage(value, t["z"][...]), t["y_high"][...], t["y_low"][...])
    total[...] = (x_stage(value, t["x"][...]) * own).reshape(3, G, WIDE)

    def forward(z, carry):
        @pl.when(z == 2)
        def _():
            arrive(fields.at[3 - core, z], field_recv.at[2 - core, z])

        arrive(fields.at[1, z], field_recv.at[0, z])
        arrive(fields.at[2 + core, z], field_recv.at[1 + core, z])
        arrive(fields.at[4, z], field_recv.at[3, z])
        value = jnp.concatenate([fields[0, z] * fields[slot, z] for slot in range(1, 5)], axis=0)
        value = y_stage(x_stage(value, t["x"][...]), t["y_high"][...], t["y_low"][...])
        for i in range(4):
            work[i, z] = value[G * i : G * (i + 1)]
        return carry

    lax.fori_loop(0, 3, forward, 0)
    value = z_stage(work[...].reshape(4 * ROWS, WIDE), t["z"][...])
    value = value * jnp.concatenate([t["kernel"][...]] * 4, axis=0)
    work[...] = z_stage(value, t["z"][...]).reshape(4, 3, G, WIDE)

    def result_copy(z, owner):
        batch = (member + OWNERS - owner) % OWNERS // 2
        source, target = found.at[z, owner], back.at[member, z]
        either(owner == stick, (owner, group), source, target, out_send.at[0], out_recv.at[batch])

    def backward(z, carry):
        value = jnp.concatenate([work[i, z] for i in range(4)], axis=0)
        value = x_stage(y_stage(value, t["y_high"][...], t["y_low"][...]), t["x"][...])
        field = total[z]
        for i in range(4):
            field = field + value[G * i : G * (i + 1)] * fields[i + 1, z]
        both = y_stage(left_product(t["x_out"][...], field), t["y_high"][...], t["y_low"][...])
        plus, minus = [[both[a : a + G, 128 * y : 128 * (y + 1)] for y in range(6)] for a in (0, G)]
        real = [a + b for a, b in zip(minus, reflected(plus))]
        imag = [a - b for a, b in zip(reflected(minus), plus)]
        for i, part in enumerate((real, imag)):
            high, low = split(jnp.concatenate(part, axis=0).T)
            turned[128 * i : 128 * (i + 1), : 6 * G] = high
            turned[128 * i : 128 * (i + 1), 6 * G :] = low

        def pick(step, carry):
            owners = [(member + OWNERS - 2 * step - i) % OWNERS for i in range(2)]
            row, span = slot_places(jnp.concatenate([columns[owner] for owner in owners], axis=1))
            hot = one_hot(row)
            picked = dot(turned[...], jnp.concatenate([hot, hot], axis=0))
            rows = []
            for i in range(2):
                value = jnp.zeros((16, 2 * CAP), F32)
                for g in range(8):
                    start = 128 * i + 16 * g
                    value = value + jnp.where(span == g, picked[start : start + 16], 0.0)
                rows.append(value)
            result = jnp.concatenate(rows, axis=0)
            for i, owner in enumerate(owners):
                found[z, owner] = result[:, CAP * i : CAP * (i + 1)]
                result_copy(z, owner)
            return carry

        lax.fori_loop(0, OWNERS // 2, pick, 0)
        return carry

    lax.fori_loop(0, 3, backward, 0)

    def from_planes(step, carry):
        bands = [(stick + 2 * step + i) % OWNERS for i in range(2)]
        arrive(back.at[pl.ds(0, 2)], out_recv.at[step])
        pair = jnp.concatenate([back[band_index].reshape(2 * G, CAP) for band_index in bands], axis=1)
        pair = left_product(t["z_out"][...], pair)
        for i, band_index in enumerate(bands):
            ready[band_index] = pair[:, CAP * i : CAP * (i + 1)]
            pltpu.make_async_copy(ready.at[band_index], out.at[band_index], out_store.at[0]).start()
        return carry

    lax.fori_loop(0, OWNERS // 2, from_planes, 0)
    arrive(fields.at[pl.ds(0, 4)], field_send.at[0])

    @pl.when(home)
    def _():
        arrive(sent.at[pl.ds(0, OWNERS - 1)], in_send.at[0])
        arrive(columns.at[pl.ds(0, OWNERS - 1)], label_send.at[0])
        arrive(found.at[:, pl.ds(0, OWNERS - 1)], out_send.at[0])

    @pl.when(jnp.logical_not(home))
    def _():
        arrive(sent, in_send.at[0])
        arrive(columns, label_send.at[0])
        arrive(found, out_send.at[0])

    pltpu.make_async_copy(ready, out, out_store.at[0]).wait()


def on_device(sticks, stick_columns):
    tables = [jnp.asarray(TABLES[name]) for name in STAGES]
    anywhere, hbm = pl.BlockSpec(memory_space=pl.ANY), pl.BlockSpec(memory_space=pltpu.HBM)
    dma = pltpu.SemaphoreType.DMA
    result = pl.pallas_call(
        exchange_kernel,
        out_shape=jax.ShapeDtypeStruct((OWNERS, 2 * G, CAP), F32),
        in_specs=[hbm] * (2 + len(tables)),
        out_specs=anywhere,
        scratch_shapes=[pltpu.VMEM(t.shape, t.dtype) for t in tables]
        + [
            pltpu.VMEM((OWNERS, 2 * G, CAP), F32),
            pltpu.VMEM((OWNERS, 2 * G, CAP), F32),
            pltpu.VMEM((3, OWNERS, 32, CAP), F32),
            pltpu.VMEM((OWNERS, 1, CAP), jnp.int32),
            pltpu.VMEM((6 * G, 256), F32),
            pltpu.VMEM((5, 3, G, WIDE), F32),
            pltpu.VMEM((4, 3, G, WIDE), F32),
            pltpu.VMEM((3, G, WIDE), F32),
            pltpu.VMEM((256, 12 * G), BF16),
            pltpu.VMEM((3, OWNERS, 32, CAP), F32),
            pltpu.VMEM((OWNERS, 3, 32, CAP), F32),
            pltpu.VMEM((OWNERS, 2 * G, CAP), F32),
            dma((len(tables) + 1,)),
            dma((1,)),
            dma((3, 4)),
            dma((1,)),
            dma((4,)),
            dma((1,)),
            dma((4, 3)),
            dma((1,)),
            dma((OWNERS // 2,)),
            dma((1,)),
        ],
        compiler_params=pltpu.CompilerParams(collective_id=0, has_side_effects=True, vmem_limit_bytes=48 << 20),
    )(*[pltpu.with_memory_space_constraint(a, pltpu.HBM) for a in (sticks, stick_columns.reshape(1, CAP), *tables)])
    return result * np.float32(G**-1.5)


def solution(mesh):
    return jax.shard_map(
        on_device,
        mesh=mesh,
        in_specs=(P("band", None, "stick"), P("stick")),
        out_specs=P("band", None, "stick"),
        check_vma=False,
    )
```
